32 devices in a mesh: ctx: 2 (over x), tp: 4 (over y, core), dp: 4 (over z).
Axes of the slice: x: 2, y: 2, z: 4, core: 2. Of those that a mesh axis runs over, the one named last changes fastest.
Arguments:
- byte_embed: bfloat16 [8192, 1024], P(('dp', 'ctx', 'tp')), parts along dimension 0, may hold values from -6 to 6
- patch_start: int32 [8192], P(('dp', 'ctx', 'tp')), parts along dimension 0, may hold values from 0 to 1, as said below
- enc_gain: float32 [1024], replicated, may hold values from 0.1 to 1.9
- enc_qkv: bfloat16 [1024, 3072], replicated, may hold values from -4 to 4
- enc_out: bfloat16 [1024, 1024], replicated, may hold values from -0.1875 to 0.1875
- up_proj: bfloat16 [1024, 4096], P('ctx', 'tp'), may hold values from -0.1875 to 0.1875
- lat_gain: float32 [4096], replicated, may hold values from 0.1 to 1.9
- query_proj: bfloat16 [4096, 2048], P('ctx', 'tp'), may hold values from -4 to 4
- key_proj: bfloat16 [4096, 512], P('ctx', 'tp'), may hold values from -4 to 4
- value_matrix: bfloat16 [4096, 512], P('ctx', 'tp'), may hold values from -0.09375 to 0.09375
- out_proj: bfloat16 [2048, 4096], P('tp', 'ctx'), may hold values from -0.125 to 0.125
- down_proj: bfloat16 [4096, 1024], P('tp', 'ctx'), may hold values from -0.09375 to 0.09375
Outputs:
- byte_states: bfloat16 [8192, 1024], P(('dp', 'ctx', 'tp')), parts along dimension 0
The draws below stay inside these ranges and needn't reach their ends.
There are 4 independent parts, one for each index of `dp`. The reference program is written for one: setup_inputs(seed, part) draws one part's arguments, and reference() takes and returns one part's arrays. A program takes and returns all parts, laid end to end along the dimension named above; an argument that names none is the same for every part. Nothing has to cross between parts.
Inputs may be any that keep to these rules, and one draw needn't show every extreme that they name: `patch_start`: byte 0 begins a patch; every patch spans 1 to 19 bytes; each aligned group of 1024 bytes holds at most 256 patch starts, and some group holds exactly 256.
All inputs are finite; a program needn't handle non-finite values.
Results may differ from the reference program's by a relative error of at most 0.015.
Values may be sent and summed in bfloat16 or wider, within the bound.
No kernel may reach another device: no remote copies, remote signals or barrier semaphores. Data moves between devices by JAX's collectives and lax.ppermute only.
A program may use at most 128 MiB of HBM per device.

```python
import math
import jax
import jax.numpy as jnp
from jax import lax

DB = 1024
BH = 16
HB = 64
LATENT_WIDTH = 4096
QUERY_HEADS = 16
KEYVALUE_HEADS = 4
HEAD_SIZE = 128
WIN = 512
BYTE_DEV = 256
GROUP = 1024
CAP = 256
BYTES = 2048
SLOTS = 512
N_CTX = 2


def draw_patch_start(key, part):
    key_prob, key_full, key_roll, key_place = jax.random.split(jax.random.fold_in(key, 7), 4)
    quads = BYTES // 4
    quad_index = jnp.arange(quads, dtype=jnp.int32)
    quad_group = quad_index // CAP
    chance = jax.random.randint(key_prob, (N_CTX,), 600, 1001)
    full_group = jax.random.randint(key_full, (), 0, N_CTX)
    chance = jnp.where(jnp.arange(N_CTX, dtype=jnp.int32) == full_group, 1000, chance)
    roll = jax.random.randint(key_roll, (quads,), 0, 1000)
    present = (roll < chance[quad_group]) | (quad_index % 4 == 0)
    place = jax.random.randint(key_place, (quads,), 0, 4)
    place = jnp.where(quad_index == 0, 0, place)
    marks = (jnp.arange(4, dtype=jnp.int32)[None, :] == place[:, None]) & present[:, None]
    return marks.reshape(BYTES).astype(jnp.int32)


def draw_byte_embed(key, part):
    key_drawn = jax.random.fold_in(jax.random.fold_in(key, 11), 0)
    simple_sample = jax.random.normal(key_drawn, (BYTES, DB), jnp.float32)
    return jnp.clip(simple_sample, -6.0, 6.0).astype(jnp.bfloat16)


def draw_enc_qkv(key, part):
    key_drawn = jax.random.fold_in(jax.random.fold_in(key, 13), 0)
    simple_sample = jax.random.normal(key_drawn, (DB, 3 * DB), jnp.float32) / math.sqrt(DB)
    return jnp.clip(simple_sample, -4.0, 4.0).astype(jnp.bfloat16)


def draw_query_proj(key, part):
    simple_sample = jax.random.normal(jax.random.fold_in(key, 31), (LATENT_WIDTH, QUERY_HEADS * HEAD_SIZE), jnp.float32) / math.sqrt(LATENT_WIDTH)
    return jnp.clip(simple_sample, -4.0, 4.0).astype(jnp.bfloat16)


def draw_key_proj(key, part):
    simple_sample = jax.random.normal(jax.random.fold_in(key, 37), (LATENT_WIDTH, KEYVALUE_HEADS * HEAD_SIZE), jnp.float32) / math.sqrt(LATENT_WIDTH)
    return jnp.clip(simple_sample, -4.0, 4.0).astype(jnp.bfloat16)


def steps_of(stream_key, dims, cuts, smallest, high):
    loudness = 1.0
    for axis_at, blocks in cuts:
        draws = jax.random.uniform(jax.random.fold_in(jax.random.fold_in(stream_key, 6), axis_at), (blocks,), jnp.float32, smallest / len(cuts), high / len(cuts))
        loudness = loudness * jnp.repeat(jnp.exp(draws), dims[axis_at] // blocks).reshape((-1,) + (1,) * (len(dims) - 1 - axis_at))
    return loudness


def noise(own_key, shape, deviation, most, pieces=(), kind=jnp.bfloat16):
    entries = jax.random.normal(own_key, shape, jnp.float32) * deviation
    if len(pieces) > 0:
        entries = steps_of(own_key, shape, pieces, -0.22, 0.18) * entries
    return jnp.clip(entries, min=-most, max=most).astype(kind)


def setup_inputs(seed: int = 0, part: int = 0) -> dict:
    seeds = jax.random.split(jax.random.key(seed), 13)
    part_splits = jax.random.split(jax.random.fold_in(seeds[12], part), 13)
    return {
        "byte_embed": draw_byte_embed(jax.random.fold_in(jax.random.fold_in(seeds[12], part), 71), part),
        "patch_start": draw_patch_start(jax.random.fold_in(jax.random.fold_in(seeds[12], part), 71), part),
        "enc_gain": jnp.clip(1.0 + 0.18 * jax.random.normal(seeds[2], (DB,), jnp.float32), 0.1, 1.9),
        "enc_qkv": draw_enc_qkv(jax.random.fold_in(seeds[12], 71), part),
        "enc_out": noise(seeds[4], (DB, DB), DB ** -0.5, 0.1875),
        "up_proj": noise(seeds[5], (DB, LATENT_WIDTH), DB ** -0.5, 0.1875, ((0, 2), (1, 4))),
        "lat_gain": jnp.clip(1.0 + 0.18 * jax.random.normal(seeds[6], (LATENT_WIDTH,), jnp.float32), 0.1, 1.9),
        "query_proj": draw_query_proj(jax.random.fold_in(seeds[12], 71), part),
        "key_proj": draw_key_proj(jax.random.fold_in(seeds[12], 71), part),
        "value_matrix": noise(seeds[9], (LATENT_WIDTH, KEYVALUE_HEADS * HEAD_SIZE), LATENT_WIDTH ** -0.5, 0.09375, ((0, 2), (1, 4))),
        "out_proj": noise(seeds[10], (QUERY_HEADS * HEAD_SIZE, LATENT_WIDTH), (QUERY_HEADS * HEAD_SIZE) ** -0.5, 0.125, ((0, 4), (1, 2))),
        "down_proj": noise(seeds[11], (LATENT_WIDTH, DB), LATENT_WIDTH ** -0.5, 0.09375, ((0, 4), (1, 2))),
    }


EPS = 1e-05

def rms_scale(values, gain):
    floats = values.astype(jnp.float32)
    return floats * lax.rsqrt(lax.optimization_barrier(jnp.mean(floats * floats, axis=-1, keepdims=True)) + EPS) * gain

def window_attend(query, keys, values, first):
    n_query = query.shape[0]
    n_key = keys.shape[0]
    qh = query.reshape(n_query, BH, HB).astype(jnp.float32)
    kh = keys.reshape(n_key, BH, HB).astype(jnp.float32)
    vh = values.reshape(n_key, BH, HB).astype(jnp.float32)
    scores = jnp.einsum('qhd,khd->hqk', qh, kh) / jnp.sqrt(jnp.float32(HB))
    q_pos = first + jnp.arange(n_query, dtype=jnp.int32)
    k_pos = first - (n_key - n_query) + jnp.arange(n_key, dtype=jnp.int32)
    allowed = (k_pos[None, :] <= q_pos[:, None]) & (k_pos[None, :] > q_pos[:, None] - WIN) & (k_pos[None, :] >= 0)
    scores = jnp.where(allowed[None], scores, jnp.float32(-1e+30))
    peak = lax.optimization_barrier(jnp.max(scores, axis=-1, keepdims=True))
    expo = jnp.where(allowed[None], jnp.exp(scores - peak), jnp.float32(0.0))
    total = lax.optimization_barrier(jnp.sum(expo, axis=-1, keepdims=True))
    weights = expo.astype(jnp.bfloat16).astype(jnp.float32)
    mixed = jnp.einsum('hqk,khd->hqd', weights, vh) / total
    return jnp.transpose(mixed, (1, 0, 2)).reshape(n_query, BH * HB).astype(jnp.bfloat16)

def reference(byte_embed, patch_start, enc_gain, enc_qkv, enc_out, up_proj, lat_gain, query_proj, key_proj, value_matrix, out_proj, down_proj):
    normed = rms_scale(byte_embed, enc_gain).astype(jnp.bfloat16)
    qkv = jnp.dot(normed, enc_qkv, preferred_element_type=jnp.float32).astype(jnp.bfloat16)
    query = qkv[:, :DB]
    keys = qkv[:, DB:2 * DB]
    values = qkv[:, 2 * DB:]
    padding = jnp.zeros((2 * BYTE_DEV, DB), jnp.bfloat16)
    key_pad = jnp.concatenate([padding, keys], axis=0)
    value_pad = jnp.concatenate([padding, values], axis=0)

    def one_block(index):
        begin = index * BYTE_DEV
        q_block = lax.dynamic_slice_in_dim(query, begin, BYTE_DEV, 0)
        k_block = lax.dynamic_slice_in_dim(key_pad, begin, 3 * BYTE_DEV, 0)
        v_block = lax.dynamic_slice_in_dim(value_pad, begin, 3 * BYTE_DEV, 0)
        return window_attend(q_block, k_block, v_block, begin)
    blocks = jnp.arange(BYTES // BYTE_DEV, dtype=jnp.int32)
    context = lax.map(one_block, blocks).reshape(BYTES, DB)
    hidden = (byte_embed.astype(jnp.float32) + jnp.dot(context, enc_out, preferred_element_type=jnp.float32)).astype(jnp.bfloat16)
    position = jnp.arange(BYTES, dtype=jnp.int32)
    group = position // GROUP
    running = jnp.cumsum(patch_start).astype(jnp.int32)
    before = running - patch_start
    base = before[jnp.arange(N_CTX, dtype=jnp.int32) * GROUP]
    slot = before - base[group]
    begin_row = jnp.where(patch_start == 1, group * CAP + slot, -1).astype(jnp.int32)
    row = lax.cummax(begin_row, axis=0)
    sums = jax.ops.segment_sum(hidden.astype(jnp.float32), row, num_segments=SLOTS)
    counts = jax.ops.segment_sum(jnp.ones((BYTES,), jnp.float32), row, num_segments=SLOTS)
    pooled = (sums / jnp.maximum(counts, 1.0)[:, None]).astype(jnp.bfloat16)
    latent = jnp.dot(pooled, up_proj, preferred_element_type=jnp.float32).astype(jnp.bfloat16)
    lnorm = rms_scale(latent, lat_gain).astype(jnp.bfloat16)
    q_all = jnp.dot(lnorm, query_proj, preferred_element_type=jnp.float32).astype(jnp.bfloat16)
    k_all = jnp.dot(lnorm, key_proj, preferred_element_type=jnp.float32).astype(jnp.bfloat16)
    v_all = jnp.dot(lnorm, value_matrix, preferred_element_type=jnp.float32).astype(jnp.bfloat16)
    used = counts > 0.0
    rows = jnp.arange(SLOTS, dtype=jnp.int32)
    allowed = used[None, :] & (rows[None, :] <= rows[:, None])

    def one_head(head_number):
        keyvalue_head = head_number // (QUERY_HEADS // KEYVALUE_HEADS)
        q_head = lax.dynamic_slice_in_dim(q_all, head_number * HEAD_SIZE, HEAD_SIZE, 1).astype(jnp.float32)
        k_head = lax.dynamic_slice_in_dim(k_all, keyvalue_head * HEAD_SIZE, HEAD_SIZE, 1).astype(jnp.float32)
        v_head = lax.dynamic_slice_in_dim(v_all, keyvalue_head * HEAD_SIZE, HEAD_SIZE, 1).astype(jnp.float32)
        scores = jnp.dot(q_head, k_head.T, precision=lax.Precision.HIGHEST) / jnp.sqrt(jnp.float32(HEAD_SIZE))
        scores = jnp.where(allowed, scores, jnp.float32(-1e+30))
        peak = lax.optimization_barrier(jnp.max(scores, axis=-1, keepdims=True))
        expo = jnp.where(allowed, jnp.exp(scores - peak), jnp.float32(0.0))
        total = lax.optimization_barrier(jnp.sum(expo, axis=-1, keepdims=True))
        weights = expo.astype(jnp.bfloat16).astype(jnp.float32)
        return (jnp.dot(weights, v_head, precision=lax.Precision.HIGHEST) / total).astype(jnp.bfloat16)
    heads = lax.map(one_head, jnp.arange(QUERY_HEADS, dtype=jnp.int32))
    attn = jnp.transpose(heads, (1, 0, 2)).reshape(SLOTS, QUERY_HEADS * HEAD_SIZE)
    latent_out = (latent.astype(jnp.float32) + jnp.dot(attn, out_proj, preferred_element_type=jnp.float32)).astype(jnp.bfloat16)
    patch_out = jnp.dot(latent_out, down_proj, preferred_element_type=jnp.float32).astype(jnp.bfloat16)
    return (hidden.astype(jnp.float32) + patch_out[row].astype(jnp.float32)).astype(jnp.bfloat16)
```

```python
import functools

import jax
import jax.numpy as jnp
from jax import lax
from jax.experimental import pallas as pl
from jax.experimental.pallas import tpu as pltpu
from jax.sharding import PartitionSpec as P

HB = 64
HEAD_SIZE = 128
WIN = 512
EPS = 1e-05
LEAD = 32
NEG = -1e30
F32 = jnp.float32
BF16 = jnp.bfloat16


def dot(a, b):
    return jnp.dot(a, b, preferred_element_type=F32)


def dot_nt(a, b):
    return lax.dot_general(a, b, (((1,), (1,)), ((), ())), preferred_element_type=F32)


def normed_rows(x, gain):
    floats = x.astype(F32)
    scale = lax.rsqrt(jnp.mean(floats * floats, axis=-1, keepdims=True) + EPS)
    return (floats * scale * gain).astype(BF16)


def call(body, ids, args, in_specs, outs, out_specs=None, grid=(1,), scratch=(), cost=None, name=None):
    specs = []
    for arg, spec in zip(args, in_specs):
        if spec is None:
            spec = pl.BlockSpec(arg.shape, functools.partial(lambda nd, *_: (0,) * nd, arg.ndim))
        specs.append(spec)
    if out_specs is None:
        out_specs = [
            pl.BlockSpec(o.shape, functools.partial(lambda nd, *_: (0,) * nd, len(o.shape))) for o in outs
        ]
    flops, nbytes = cost if cost is not None else (1e9, 4e6)
    return pl.pallas_call(
        body,
        out_shape=outs,
        grid_spec=pltpu.PrefetchScalarGridSpec(
            num_scalar_prefetch=1,
            grid=grid,
            in_specs=specs,
            out_specs=out_specs,
            scratch_shapes=list(scratch),
        ),
        compiler_params=pltpu.CompilerParams(dimension_semantics=("arbitrary",) * len(grid)),
        cost_estimate=pl.CostEstimate(flops=int(flops), bytes_accessed=int(nbytes), transcendentals=0),
        name=name,
    )(ids, *args)


K, A, C, Z, PREV, USED, USED_OTHER, LAST = range(8)


def qkv_kernel(ids, own, other, gain, wq, wk, wv, q_ref, k_ref, v_ref, normed):
    n = own.shape[0]

    @pl.when(pl.program_id(0) == 0)
    def _():
        k = ids[K]
        normed[pl.ds(pl.multiple_of(k * n, n), n), :] = normed_rows(own[...], gain[...])
        normed[pl.ds(pl.multiple_of((1 - k) * n, n), n), :] = normed_rows(other[...], gain[...])

    x = normed[...]
    q_ref[...] = (dot(x, wq[...]).astype(BF16).astype(F32) * (1.0 / HB**0.5)).astype(BF16)
    k_ref[...] = dot(x, wk[...]).astype(BF16)
    v_ref[...] = dot(x, wv[...]).astype(BF16)


def window_kernel(ids, own, other, gain, wk, wv, q_ref, k_ref, v_ref, o_ref, normed, kh, vh):
    n = own.shape[0]

    @pl.when(pl.program_id(0) == 0)
    def _():
        k = ids[K]
        normed[pl.ds(pl.multiple_of(k * n, n), n), :] = normed_rows(own[...], gain[...])
        normed[pl.ds(pl.multiple_of((1 - k) * n, n), n), :] = normed_rows(other[...], gain[...])

    x = normed[...]
    kh[...] = dot(x, wk[...]).astype(BF16)
    vh[...] = dot(x, wv[...]).astype(BF16)
    rows = q_ref.shape[0]
    blk = 128
    nblk = rows // blk
    bias = jnp.where(ids[PREV] == 1, 0.0, NEG).astype(F32)
    low = lax.broadcasted_iota(jnp.int32, (blk, 2 * HB), 1) < HB
    r = lax.broadcasted_iota(jnp.int32, (2 * blk, blk), 0)
    causal = lax.broadcasted_iota(jnp.int32, (2 * blk, blk), 1) <= jnp.where(r >= blk, r - blk, r)
    zero = jnp.zeros((blk, 2 * HB), BF16)
    for pair in range(q_ref.shape[1] // (2 * HB)):
        cols = slice(pair * 2 * HB, (pair + 1) * 2 * HB)
        for b in range(nblk):
            qb = q_ref[b * blk : (b + 1) * blk, cols]
            q2 = jnp.concatenate([jnp.where(low, qb, zero), jnp.where(low, zero, qb)], axis=0)
            s_own = dot_nt(q2, k_ref[: (b + 1) * blk, cols])
            s_halo = dot_nt(q2, kh[b * blk :, cols]) + bias
            diag = jnp.where(causal, s_own[:, b * blk :], s_halo[:, :blk])
            peak = jnp.max(diag, axis=-1, keepdims=True)
            if b > 0:
                peak = jnp.maximum(peak, jnp.max(s_own[:, : b * blk], axis=-1, keepdims=True))
            if b < nblk - 1:
                peak = jnp.maximum(peak, jnp.max(s_halo[:, blk:], axis=-1, keepdims=True))
            e_diag = jnp.exp(diag - peak)
            total = jnp.sum(e_diag, axis=-1, keepdims=True)
            e_own = jnp.where(causal, e_diag, 0.0).astype(BF16)
            e_halo = jnp.where(causal, 0.0, e_diag).astype(BF16)
            if b > 0:
                e = jnp.exp(s_own[:, : b * blk] - peak)
                total = total + jnp.sum(e, axis=-1, keepdims=True)
                e_own = jnp.concatenate([e.astype(BF16), e_own], axis=1)
            if b < nblk - 1:
                e = jnp.exp(s_halo[:, blk:] - peak)
                total = total + jnp.sum(e, axis=-1, keepdims=True)
                e_halo = jnp.concatenate([e_halo, e.astype(BF16)], axis=1)
            mixed = dot(e_own, v_ref[: (b + 1) * blk, cols]) + dot(e_halo, vh[b * blk :, cols])
            mixed = mixed / total
            o_ref[b * blk : (b + 1) * blk, cols] = jnp.where(low, mixed[:blk], mixed[blk:]).astype(BF16)


def hidden_kernel(ids, ctx_own, ctx_other, w_own, w_other, emb_own, emb_other, slot, h_ref, p_ref, pb_ref, acc):
    n = emb_own.shape[0]
    k = ids[K]
    acc[pl.ds(pl.multiple_of(k * n, n), n), :] = emb_own[...].astype(F32)
    acc[pl.ds(pl.multiple_of((1 - k) * n, n), n), :] = emb_other[...].astype(F32)
    mixed = dot(ctx_own[...], w_own[...]) + dot(ctx_other[...], w_other[...])
    hidden = (acc[...] + mixed).astype(BF16)
    h_ref[...] = hidden
    slots = p_ref.shape[0]
    hot = lax.broadcasted_iota(jnp.int32, (slots, 2 * n), 0) == slot[...]
    part = dot(hot.astype(F32).astype(BF16), hidden)
    p_ref[...] = part
    pb_ref[...] = part.astype(BF16)


def up_kernel(ids, half, other, w_own, w_x, w_z, o_ref, pool):
    n = half.shape[1]
    k, c, z = ids[K], ids[C], ids[Z]
    pool[:, pl.ds(pl.multiple_of(k * n, n), n)] = half[...]
    pool[:, pl.ds(pl.multiple_of((1 - k) * n, n), n)] = other[...]
    rows = w_own.shape[0]
    part = rows // 2
    own = dot(pool[:, pl.ds(pl.multiple_of(c * rows, rows), rows)], w_own[...])
    base = (1 - c) * rows
    at_x = pl.multiple_of(base + z * part, part)
    at_z = pl.multiple_of(base + (1 - z) * part, part)
    total = own + dot(pool[:, pl.ds(at_x, part)], w_x[...]) + dot(pool[:, pl.ds(at_z, part)], w_z[...])
    o_ref[...] = total.astype(BF16)


def kv_kernel(ids, l0, l1, l2, l3, gain, wk, wv, w_x, w_z, s_ref, scale_ref, kv_ref):
    n = l0.shape[1]
    t = ids[A] * 2 + ids[K]
    square = jnp.zeros((l0.shape[0], 1), F32)
    for j, piece in enumerate((l0, l1, l2, l3)):
        at = pl.multiple_of((t ^ j) * n, n)
        floats = piece[...].astype(F32)
        square = square + jnp.sum(floats * floats, axis=-1, keepdims=True)
        s_ref[:, pl.ds(at, n)] = (floats * gain[:, pl.ds(at, n)]).astype(BF16)
    scale = lax.rsqrt(square / (4 * n) + EPS)
    scale_ref[...] = jnp.broadcast_to(scale, scale_ref.shape)
    rows = wk.shape[0]
    part = rows // 2
    c, z = ids[C], ids[Z]
    mine = s_ref[:, pl.ds(pl.multiple_of(c * rows, rows), rows)]
    base = (1 - c) * rows
    rest = dot(s_ref[:, pl.ds(pl.multiple_of(base + z * part, part), part)], w_x[...]) + dot(
        s_ref[:, pl.ds(pl.multiple_of(base + (1 - z) * part, part), part)], w_z[...]
    )
    w = wk.shape[1]
    kv_ref[:, :w] = ((dot(mine, wk[...]) + rest[:, :w]) * scale).astype(BF16)
    kv_ref[:, w:] = ((dot(mine, wv[...]) + rest[:, w:]) * scale).astype(BF16)


def q_kernel(ids, s_ref, scale, w_own, x0, z0, x1, z1, q_ref):
    rows = w_own.shape[0]
    part = rows // 2
    w = x0.shape[1]
    c, z = ids[C], ids[Z]
    base = (1 - c) * rows
    mine = s_ref[:, pl.ds(pl.multiple_of(c * rows, rows), rows)]
    sx = s_ref[:, pl.ds(pl.multiple_of(base + z * part, part), part)]
    sz = s_ref[:, pl.ds(pl.multiple_of(base + (1 - z) * part, part), part)]
    for j, (wx, wz) in enumerate(((x0, z0), (x1, z1))):
        total = dot(mine, w_own[:, j * w : (j + 1) * w]) + dot(sx, wx[...]) + dot(sz, wz[...])
        q_ref[:, j * w : (j + 1) * w] = (total * scale[:, :1]).astype(BF16)


def latent_attend(ids, q_ref, kv_own, kv_other, attn):
    slots = q_ref.shape[0]
    d = HEAD_SIZE
    row = lax.broadcasted_iota(jnp.int32, (slots, slots), 0)
    col = lax.broadcasted_iota(jnp.int32, (slots, slots), 1)
    ok_own = (col <= row) & (col < ids[USED])
    ok_other = col < jnp.where(ids[C] == 1, ids[USED_OTHER], 0)
    scale = 1.0 / HEAD_SIZE**0.5
    for h in range(q_ref.shape[1] // d):
        qh = q_ref[:, h * d : (h + 1) * d]
        s0 = jnp.where(ok_own, dot_nt(qh, kv_own[:, :d]) * scale, NEG)
        s1 = jnp.where(ok_other, dot_nt(qh, kv_other[:, :d]) * scale, NEG)
        peak = jnp.maximum(jnp.max(s0, axis=-1, keepdims=True), jnp.max(s1, axis=-1, keepdims=True))
        e0 = jnp.where(ok_own, jnp.exp(s0 - peak), 0.0)
        e1 = jnp.where(ok_other, jnp.exp(s1 - peak), 0.0)
        total = jnp.sum(e0, axis=-1, keepdims=True) + jnp.sum(e1, axis=-1, keepdims=True)
        mixed = dot(e0.astype(BF16), kv_own[:, d:]) + dot(e1.astype(BF16), kv_other[:, d:])
        attn[:, h * d : (h + 1) * d] = (mixed / total).astype(BF16)


def out_kernel(ids, q_ref, kv_own, kv_other, w_own, x0, z0, x1, z1, far_send, far_keep, near_send, near_keep, attn):
    latent_attend(ids, q_ref, kv_own, kv_other, attn)
    w = x0.shape[1]
    part = x0.shape[0]
    k, a, c, z = ids[K], ids[A], ids[C], ids[Z]
    for chip, keep, send in ((1 - a, far_keep, far_send), (a, near_keep, near_send)):

        def store(j, value, keep=keep, send=send):
            @pl.when(k == j)
            def _():
                keep[...] = value.astype(keep.dtype)

            @pl.when(k != j)
            def _():
                send[...] = value.astype(send.dtype)

        @pl.when(chip == c)
        def _(store=store):
            for j in range(2):
                store(j, dot(attn[...], w_own[:, j * w : (j + 1) * w]))

        @pl.when(chip != c)
        def _(store=store):
            ax = attn[:, pl.ds(pl.multiple_of(z * part, part), part)]
            az = attn[:, pl.ds(pl.multiple_of((1 - z) * part, part), part)]
            for j, (wx, wz) in enumerate(((x0, z0), (x1, z1))):
                store(j, dot(ax, wx[...]) + dot(az, wz[...]))


def down_kernel(ids, base, recv, w_own, w_x, w_z, send, keep, lo):
    k, c, z = ids[K], ids[C], ids[Z]
    lo[...] = (base[...] + recv[...].astype(F32)).astype(BF16)
    part = w_x.shape[0]
    own = dot(lo[...], w_own[...])
    rest = dot(lo[:, pl.ds(pl.multiple_of(z * part, part), part)], w_x[...]) + dot(
        lo[:, pl.ds(pl.multiple_of((1 - z) * part, part), part)], w_z[...]
    )

    @pl.when(c == k)
    def _():
        keep[...] = own
        send[...] = rest.astype(BF16)

    @pl.when(c != k)
    def _():
        keep[...] = rest
        send[...] = own.astype(BF16)


def final_kernel(ids, hidden, patch, recv, slot, carry0, carry1, o_ref):
    patch_out = (patch[...] + recv[...].astype(F32)).astype(BF16)
    n = hidden.shape[0]
    hot = lax.broadcasted_iota(jnp.int32, (n, patch.shape[0]), 1) == slot[...]
    spread = dot(hot.astype(F32).astype(BF16), patch_out)
    carried = (carry0[...] + carry1[...].astype(F32)).astype(BF16).astype(F32)
    lead = (slot[...] < 0).astype(F32)
    o_ref[...] = (hidden[...].astype(F32) + spread + lead * carried).astype(BF16)


def shape(dims, dtype=BF16):
    return jax.ShapeDtypeStruct(dims, dtype)


def local(
    byte_embed,
    patch_start,
    enc_gain,
    enc_qkv,
    enc_out,
    up_proj,
    lat_gain,
    query_proj,
    key_proj,
    value_matrix,
    out_proj,
    down_proj,
):
    nbytes, width = byte_embed.shape
    n_tp = lax.axis_size("tp")
    n_ctx = lax.axis_size("ctx")
    n_dp = lax.axis_size("dp")
    half = width // 2
    slots = n_tp * nbytes // 4
    t = lax.axis_index("tp")
    c = lax.axis_index("ctx")
    zp = lax.axis_index("dp") % 2
    a, k = t // 2, t % 2
    where_k = lambda first, second: jnp.where(k == 0, first, second)

    def swap(x):
        return lax.ppermute(x, "tp", [(i, i ^ 1) for i in range(n_tp)])

    def cross(x):
        return lax.ppermute(x, "tp", [(i, i ^ 2) for i in range(n_tp)])

    def forward(x):
        n = n_ctx * n_tp
        return lax.ppermute(x, ("ctx", "tp"), [(i, i + 2) for i in range(n - 2)])

    paired = n_ctx == 2

    emb_halo = forward(byte_embed)
    emb_other = swap(byte_embed)
    emb_halo_other = swap(emb_halo)

    start_other = swap(patch_start)
    chip_start = where_k(
        jnp.concatenate([patch_start, start_other]), jnp.concatenate([start_other, patch_start])
    )
    chip_far = cross(chip_start)
    group_start = jnp.where(
        a == 0, jnp.concatenate([chip_start, chip_far]), jnp.concatenate([chip_far, chip_start])
    )
    if paired:
        flip = lax.ppermute(group_start, "ctx", [(0, 1), (1, 0)])
        all_start = jnp.where(c == 0, jnp.stack([group_start, flip]), jnp.stack([flip, group_start]))
    else:
        all_start = lax.all_gather(group_start, "ctx", axis=0, tiled=False)
    used = jnp.sum(all_start, axis=1)
    group_slot = jnp.cumsum(group_start) - 1
    chip_slot = lax.dynamic_slice_in_dim(group_slot, a * 2 * nbytes, 2 * nbytes, 0)
    following = lax.dynamic_index_in_dim(all_start, jnp.minimum(c + 1, n_ctx - 1), 0, keepdims=False)
    lead_next = (jnp.cumsum(following[:LEAD]) == 0) & (c + 1 < n_ctx)
    own_used = used[c]
    last = own_used - 1
    rows_iota = jnp.arange(slots, dtype=jnp.int32)
    count = jnp.sum((group_slot[None, :] == rows_iota[:, None]).astype(F32), axis=1)
    count = count + jnp.where(rows_iota == last, jnp.sum(lead_next.astype(F32)), 0.0)
    share = jnp.maximum(count, 1.0)
    other_used = used[(c + 1) % n_ctx]
    one = lambda x: x.astype(jnp.int32)
    place = jnp.stack([one(k), one(a), one(c), one(zp), one(c * 2 + a > 0)])
    ids = jnp.concatenate([place, jnp.stack([own_used, other_used, last])])

    if paired:
        n_half = lambda w: w.shape[0] // 2
        mine = lambda w: lax.dynamic_slice_in_dim(w, zp * n_half(w), n_half(w), 0)
        q_half = mine(query_proj)
        o_half = mine(out_proj)
        qn, on = q_half.shape[1] // 2, o_half.shape[1] // 2
        pieces = [
            mine(up_proj),
            jnp.concatenate([mine(key_proj), mine(value_matrix)], axis=1),
            q_half[:, :qn],
            q_half[:, qn:],
            o_half[:, :on],
            o_half[:, on:],
            mine(down_proj),
        ]
        flip = lambda x: lax.ppermute(x, "ctx", [(0, 1), (1, 0)])
        pair = lambda x: lax.ppermute(x, "dp", [(i, i ^ 1) for i in range(n_dp)])
        from_x = [flip(p) for p in pieces]
        from_z = [pair(p) for p in from_x]

    gain = enc_gain.reshape(1, width)
    cb = 256
    nb = half // cb
    col = lambda part: pl.BlockSpec((width, cb), lambda p, ids: (0, part * 2 * nb + ids[K] * nb + p))
    head_out = pl.BlockSpec((2 * nbytes, cb), lambda p, ids: (0, p))
    q, kk, v = call(
        qkv_kernel,
        place,
        (byte_embed, emb_other, gain, enc_qkv, enc_qkv, enc_qkv),
        (None, None, None, col(0), col(1), col(2)),
        [shape((2 * nbytes, half))] * 3,
        [head_out] * 3,
        grid=(nb,),
        scratch=[pltpu.VMEM((2 * nbytes, width), BF16)],
        cost=(2 * 2 * nbytes * width * 3 * half, 6e6),
        name="qkv",
    )
    context = call(
        window_kernel,
        place,
        (emb_halo, emb_halo_other, gain, enc_qkv, enc_qkv, q, kk, v),
        (None, None, None, col(1), col(2), head_out, head_out, head_out),
        [shape((2 * nbytes, half))],
        [head_out],
        grid=(nb,),
        scratch=[
            pltpu.VMEM((2 * nbytes, width), BF16),
            pltpu.VMEM((2 * nbytes, cb), BF16),
            pltpu.VMEM((2 * nbytes, cb), BF16),
        ],
        cost=(8e9, 6e6),
        name="window",
    )[0]
    context_other = swap(context)
    block = lambda r, cidx, rows=half: pl.BlockSpec(
        (rows, half), lambda p, ids: (r(ids), cidx(ids))
    )
    core = lambda ids: ids[K]
    not_core = lambda ids: 1 - ids[K]
    zero = lambda ids: 0
    hidden, part_sum, part_send = call(
        hidden_kernel,
        place,
        (context, context_other, enc_out, enc_out, byte_embed, emb_other, chip_slot.reshape(1, -1)),
        (None, None, block(core, core), block(not_core, core), block(zero, core, nbytes), block(zero, core, nbytes), None),
        [shape((2 * nbytes, half)), shape((slots, half), F32), shape((slots, half))],
        scratch=[pltpu.VMEM((2 * nbytes, half), F32)],
        cost=(1.5e9, 4e6),
        name="hidden",
    )

    lead_rows = hidden[:LEAD]
    back = lambda to: [(g * n_tp + j, (g - 1) * n_tp + to * 2 + j) for g in range(1, n_ctx) for j in range(2)]
    lead0 = lax.ppermute(lead_rows, ("ctx", "tp"), back(0))
    lead1 = lax.ppermute(lead_rows, ("ctx", "tp"), back(1))
    part_recv = cross(part_send)
    lead_sum = dot(lead_next.astype(BF16)[None, :], jnp.where(a == 0, lead0, lead1))
    sums = part_sum + part_recv.astype(F32) + jnp.where(rows_iota == last, 1.0, 0.0)[:, None] * lead_sum
    pooled = (sums / share[:, None]).astype(BF16)
    pooled_other = swap(pooled)

    out_cols = out_proj.shape[1] * n_ctx // n_tp
    lat_cols = up_proj.shape[1]
    if paired:
        latent = call(
            up_kernel,
            place,
            (pooled, pooled_other, up_proj, from_x[0], from_z[0]),
            (None,) * 5,
            [shape((slots, lat_cols))],
            scratch=[pltpu.VMEM((slots, width), BF16)],
            cost=(0.6e9, 4e6),
            name="up",
        )[0]
    else:
        whole = where_k(
            jnp.concatenate([pooled, pooled_other], axis=1), jnp.concatenate([pooled_other, pooled], axis=1)
        )
        latent = dot(whole, lax.all_gather(up_proj, "ctx", axis=0, tiled=True)).astype(BF16)

    l2 = cross(latent)
    l1 = swap(latent)
    l3 = swap(l2)
    heads = query_proj.shape[1] // HEAD_SIZE
    kv_w = key_proj.shape[1]
    out_shapes = [
        shape((slots, out_cols)),
        shape((slots, out_cols), F32),
        shape((slots, out_cols)),
        shape((slots, out_cols), F32),
    ]
    if paired:
        scaled, scale, kv = call(
            kv_kernel,
            place,
            (latent, l1, l2, l3, lat_gain.reshape(1, -1), key_proj, value_matrix, from_x[1], from_z[1]),
            (None,) * 9,
            [shape((slots, 4 * lat_cols)), shape((slots, 128), F32), shape((slots, 2 * kv_w))],
            cost=(1e9, 6e6),
            name="kv",
        )
        kv_far = lax.ppermute(kv, "ctx", [(0, 1), (1, 0)])
        query = call(
            q_kernel,
            place,
            (scaled, scale, query_proj, from_x[2], from_z[2], from_x[3], from_z[3]),
            (None,) * 7,
            [shape((slots, heads * HEAD_SIZE))],
            cost=(1.2e9, 6e6),
            name="q",
        )[0]
        far_send, far_keep, near_send, near_keep = call(
            out_kernel,
            ids,
            (query, kv, kv_far, out_proj, from_x[4], from_z[4], from_x[5], from_z[5]),
            (None,) * 8,
            out_shapes,
            scratch=[pltpu.VMEM((slots, heads * HEAD_SIZE), BF16)],
            cost=(2e9, 6e6),
            name="out",
        )
    else:
        stacked = jnp.stack([latent, l1, l2, l3])
        lat = jnp.concatenate(
            [lax.dynamic_index_in_dim(stacked, t ^ i, 0, keepdims=False) for i in range(n_tp)], axis=1
        )
        lnorm = normed_rows(lat, lat_gain)
        gather = lambda w, axis: lax.all_gather(w, "ctx", axis=axis, tiled=True)
        query = dot(lnorm, gather(query_proj, 0)).astype(BF16)
        kv = jnp.concatenate([dot(lnorm, gather(key_proj, 0)), dot(lnorm, gather(value_matrix, 0))], axis=1)
        keys = gather(kv.astype(BF16), 0)
        key_rows = jnp.arange(keys.shape[0], dtype=jnp.int32)
        allowed = (key_rows % slots < used[key_rows // slots])[None, :] & (
            key_rows[None, :] <= (c * slots + rows_iota)[:, None]
        )
        qh = jnp.transpose(query.reshape(slots, heads, HEAD_SIZE), (1, 0, 2))
        scores = jnp.einsum("hqd,kd->hqk", qh, keys[:, :kv_w], preferred_element_type=F32) / HEAD_SIZE**0.5
        scores = jnp.where(allowed[None], scores, NEG)
        expo = jnp.where(allowed[None], jnp.exp(scores - jnp.max(scores, axis=-1, keepdims=True)), 0.0)
        total = jnp.sum(expo, axis=-1, keepdims=True)
        mixed = jnp.einsum("hqk,kd->hqd", expo.astype(BF16), keys[:, kv_w:], preferred_element_type=F32) / total
        attn = jnp.transpose(mixed, (1, 0, 2)).reshape(slots, heads * HEAD_SIZE).astype(BF16)
        full = dot(attn, gather(out_proj, 1))
        pick = lambda j: lax.dynamic_slice_in_dim(full, (t ^ j) * out_cols, out_cols, 1)
        near_keep, near_send, far_keep, far_send = pick(0), pick(1).astype(BF16), pick(2), pick(3).astype(BF16)

    far = (far_keep + swap(far_send).astype(F32)).astype(BF16)
    far_recv = cross(far)
    base = latent.astype(F32) + near_keep + swap(near_send).astype(F32)
    if paired:
        down_send, down_keep = call(
            down_kernel,
            place,
            (base, far_recv, down_proj, from_x[6], from_z[6]),
            (None,) * 5,
            [shape((slots, half)), shape((slots, half), F32)],
            scratch=[pltpu.VMEM((slots, lat_cols), BF16)],
            cost=(0.6e9, 4e6),
            name="down",
        )
    else:
        latent_out = (base + far_recv.astype(F32)).astype(BF16)
        full = dot(latent_out, gather(down_proj, 1))
        down_keep = lax.dynamic_slice_in_dim(full, k * half, half, 1)
        down_send = lax.dynamic_slice_in_dim(full, (1 - k) * half, half, 1).astype(BF16)

    chip_sum = down_keep + swap(down_send).astype(F32)
    chip_low = chip_sum.astype(BF16)
    sum_recv = cross(chip_low)
    trailing = lax.dynamic_slice_in_dim(chip_low, last, 1, 0)
    ahead = lambda at: [(g * n_tp + at * 2 + j, (g + 1) * n_tp + j) for g in range(n_ctx - 1) for j in range(2)]
    carry0 = lax.ppermute(trailing, ("ctx", "tp"), ahead(0))
    carry1 = lax.ppermute(trailing, ("ctx", "tp"), ahead(1))
    states = call(
        final_kernel,
        place,
        (hidden, chip_sum, sum_recv, chip_slot.reshape(-1, 1), carry0.astype(F32), carry1),
        (None,) * 6,
        [shape((2 * nbytes, half))],
        cost=(0.4e9, 3e6),
        name="final",
    )[0]
    kept = lax.dynamic_slice_in_dim(states, k * nbytes, nbytes, 0)
    got = swap(lax.dynamic_slice_in_dim(states, (1 - k) * nbytes, nbytes, 0))
    return where_k(jnp.concatenate([kept, got], axis=1), jnp.concatenate([got, kept], axis=1))


def solution(mesh):
    placed = (
        P(("dp", "ctx", "tp"), None),
        P(("dp", "ctx", "tp")),
        P(),
        P(),
        P(),
        P("ctx", "tp"),
        P(),
        P("ctx", "tp"),
        P("ctx", "tp"),
        P("ctx", "tp"),
        P("tp", "ctx"),
        P("tp", "ctx"),
    )
    return jax.shard_map(
        local, mesh=mesh, in_specs=placed, out_specs=P(("dp", "ctx", "tp"), None), check_vma=False
    )
```

```python
import jax
import jax.numpy as jnp
from jax import lax
from jax.experimental import pallas as pl
from jax.experimental.pallas import tpu as pltpu
from jax.sharding import PartitionSpec as P


HB = 64
HEAD_SIZE = 128
EPS = 1e-05
LEAD = 32
NEG = -1e30
VMEM_LIMIT = 24 << 20
F32 = jnp.float32
BF16 = jnp.bfloat16


def dot(a, b):
    return jnp.dot(a, b, preferred_element_type=F32)


def dot_nt(a, b):
    return lax.dot_general(a, b, (((1,), (1,)), ((), ())), preferred_element_type=F32)


def normed_rows(x, gain):
    floats = x.astype(F32)
    scale = lax.rsqrt(jnp.mean(floats * floats, axis=-1, keepdims=True) + EPS)
    return (floats * scale * gain).astype(BF16)


def call(body, ids, args, in_specs, outs, out_specs=None, grid=(1,), scratch=(), cost=(1e7, 1e6), limit=VMEM_LIMIT):
    whole = pl.BlockSpec(memory_space=pltpu.VMEM)
    flops, nbytes = cost
    return pl.pallas_call(
        body,
        out_shape=outs,
        grid_spec=pltpu.PrefetchScalarGridSpec(
            num_scalar_prefetch=1,
            grid=grid,
            in_specs=[whole if spec is None else spec for spec in in_specs],
            out_specs=[whole] * len(outs) if out_specs is None else out_specs,
            scratch_shapes=list(scratch),
        ),
        compiler_params=pltpu.CompilerParams(
            dimension_semantics=("arbitrary",) * len(grid), vmem_limit_bytes=limit
        ),
        cost_estimate=pl.CostEstimate(flops=int(flops), bytes_accessed=int(nbytes), transcendentals=0),
    )(ids, *args)


K, A, C, Z, PREV = range(5)
USED, LAST = range(2)
SMEM_SPEC = pl.BlockSpec(memory_space=pltpu.SMEM)


def rows_at(start, n):
    return pl.ds(pl.multiple_of(start, n), n)


def halves_kernel(ids, query, out, out_rest, down, q0, q1, o0, o1, o2, o3, d):
    w = q0.shape[1]
    q0[...] = query[:, :w]
    q1[...] = query[:, w:]
    w = o0.shape[1]
    n = o1.shape[0]
    o0[...] = out[:, :w]
    o1[...] = out[:n, w:]
    o2[...] = out[n:, w:]
    o3[...] = out_rest[...]
    d[...] = down[...]


def join_kernel(ids, own, other, o_ref):
    n = own.shape[1]
    k = ids[K]
    o_ref[:, rows_at(k * n, n)] = own[...]
    o_ref[:, rows_at((1 - k) * n, n)] = other[...]


def meta_kernel(ids, mine, other, extra0, extra1, slot_row, slot_col, totals):
    n = mine.shape[1]
    a = ids[A]
    lane = 128
    upper = (
        lax.broadcasted_iota(jnp.int32, (lane, lane), 0) <= lax.broadcasted_iota(jnp.int32, (lane, lane), 1)
    ).astype(F32).astype(BF16)

    def prefix(starts):
        return dot(jnp.broadcast_to(starts, (8, lane)).astype(BF16), upper)[:1]

    row_mine, row_other = mine[...].astype(F32), other[...].astype(F32)
    total_mine, total_other = jnp.sum(row_mine), jnp.sum(row_other)
    base = jnp.zeros((1, 1), F32) + jnp.where(a == 1, total_other, 0.0)
    for j in range(n // lane):
        at = slice(j * lane, (j + 1) * lane)
        sums = prefix(row_mine[:, at]) + base
        slot_row[:, at] = sums.astype(jnp.int32) - 1
        base = sums[:, lane - 1 :]
    own_used = (total_mine + total_other).astype(jnp.int32)
    follow = (extra0[LEAD:, :] + extra1[LEAD:, :])[:1].astype(F32)
    led = prefix(follow[:, :lane])[:, :LEAD]
    leads = (led < 0.5) & (follow[:, lane : lane + 1] > 0.5)
    slot_row[:, n:] = jnp.where(leads, own_used - 1, -1)
    row = lax.broadcasted_iota(jnp.int32, (n, n), 0)
    col = lax.broadcasted_iota(jnp.int32, (n, n), 1)
    slot_col[...] = jnp.sum(jnp.where(row == col, slot_row[:, :n].astype(F32), 0.0), axis=1, keepdims=True).astype(
        jnp.int32
    )
    totals[USED] = own_used
    totals[LAST] = own_used - 1


def qkv_kernel(ids, own, other, extra0, extra1, gain, w_hbm, q_ref, kt_ref, kx_ref, v_ref, wk, wv, normed, wq, sems):
    n, width = own.shape
    half = width // 2
    k = ids[K]
    copies = []
    for part, target in ((1, wk), (2, wv), (0, wq)):
        at = pl.ds(pl.multiple_of(part * width + k * half, half), half)
        copies.append(pltpu.make_async_copy(w_hbm.at[:, at], target, sems.at[part]))
        copies[-1].start()
    normed[rows_at(k * n, n), :] = normed_rows(own[...], gain[...])
    normed[rows_at((1 - k) * n, n), :] = normed_rows(other[...], gain[...])
    normed[2 * n :, :] = normed_rows(extra0[:LEAD, :] + extra1[:LEAD, :], gain[...])
    for copy in copies:
        copy.wait()
    w = 256
    for j in range(half // w):
        at = slice(j * w, (j + 1) * w)
        keys = dot(normed[...], wk[:, at])
        kx_ref[:, at] = keys[2 * n :].astype(BF16)
        kt_ref[at, :] = jnp.transpose(keys[: 2 * n]).astype(BF16)
        v_ref[:, at] = dot(normed[...], wv[:, at]).astype(BF16)
        q_ref[:, at] = (dot(normed[...], wq[:, at]).astype(BF16).astype(F32) * (1.0 / HB**0.5)).astype(BF16)


def window_kernel(ids, own, other, gain, wk, wv, q_ref, kt_ref, kx_ref, v_ref, o_ref, normed, kht, vh):
    n = own.shape[0]
    k = ids[K]
    normed[rows_at(k * n, n), :] = normed_rows(own[...], gain[...])
    normed[rows_at((1 - k) * n, n), :] = normed_rows(other[...], gain[...])
    rows = 2 * n
    n_extra = q_ref.shape[0] - rows
    blk = 128
    lanes = 2 * HB
    nblk = rows // blk
    bias = jnp.where(ids[PREV] == 1, 0.0, NEG).astype(F32)
    low = lax.broadcasted_iota(jnp.int32, (blk, lanes), 1) < HB
    r = lax.broadcasted_iota(jnp.int32, (2 * blk, blk), 0)
    causal = lax.broadcasted_iota(jnp.int32, (2 * blk, blk), 1) <= jnp.where(r >= blk, r - blk, r)
    re = lax.broadcasted_iota(jnp.int32, (2 * n_extra, rows), 0)
    re = jnp.where(re >= n_extra, re - n_extra, re)
    ok_own = lax.broadcasted_iota(jnp.int32, (2 * n_extra, rows), 1) > re
    ok_new = lax.broadcasted_iota(jnp.int32, (2 * n_extra, n_extra), 1) <= re[:, :n_extra]

    def split(qb):
        keep = low[: qb.shape[0]]
        none = jnp.zeros_like(qb)
        return jnp.concatenate([jnp.where(keep, qb, none), jnp.where(keep, none, qb)], axis=0)

    def join(mixed):
        m = mixed.shape[0] // 2
        mixed = mixed[:, :lanes] / mixed[:, lanes:]
        return jnp.where(low[:m], mixed[:m], mixed[m:]).astype(BF16)

    def weighted(e, v):
        return dot(e.astype(BF16), jnp.concatenate([v, jnp.ones_like(v)], axis=1))

    def group(g, _):
        w = kht.shape[0]
        wide = pl.ds(pl.multiple_of(g * w, w), w)
        kht[...] = jnp.transpose(dot(normed[...], wk[:, wide])).astype(BF16)
        vh[...] = dot(normed[...], wv[:, wide]).astype(BF16)
        for pair in range(w // lanes):
            cols = pl.ds(pl.multiple_of(g * w + pair * lanes, lanes), lanes)
            part = slice(pair * lanes, (pair + 1) * lanes)
            for b in range(nblk):
                q2 = split(q_ref[b * blk : (b + 1) * blk, cols])
                s_own = dot(q2, kt_ref[cols, : (b + 1) * blk])
                s_halo = dot(q2, kht[part, b * blk :]) + bias
                diag = jnp.where(causal, s_own[:, b * blk :], s_halo[:, :blk])
                peak = jnp.max(diag, axis=-1, keepdims=True)
                if b > 0:
                    peak = jnp.maximum(peak, jnp.max(s_own[:, : b * blk], axis=-1, keepdims=True))
                if b < nblk - 1:
                    peak = jnp.maximum(peak, jnp.max(s_halo[:, blk:], axis=-1, keepdims=True))
                e_diag = jnp.exp(diag - peak)
                e_own = jnp.where(causal, e_diag, 0.0)
                e_halo = jnp.where(causal, 0.0, e_diag)
                if b > 0:
                    e_own = jnp.concatenate([jnp.exp(s_own[:, : b * blk] - peak), e_own], axis=1)
                if b < nblk - 1:
                    e_halo = jnp.concatenate([e_halo, jnp.exp(s_halo[:, blk:] - peak)], axis=1)
                mixed = weighted(e_own, v_ref[: (b + 1) * blk, cols]) + weighted(e_halo, vh[b * blk :, part])
                o_ref[b * blk : (b + 1) * blk, cols] = join(mixed)
            q2 = split(q_ref[rows:, cols])
            s_own = jnp.where(ok_own, dot(q2, kt_ref[cols, :]), NEG)
            s_new = jnp.where(ok_new, dot_nt(q2, kx_ref[:, cols]), NEG)
            peak = jnp.maximum(jnp.max(s_own, axis=-1, keepdims=True), jnp.max(s_new, axis=-1, keepdims=True))
            mixed = weighted(jnp.exp(s_own - peak), v_ref[:rows, cols]) + weighted(
                jnp.exp(s_new - peak), v_ref[rows:, cols]
            )
            o_ref[rows:, cols] = join(mixed)
        return 0

    lax.fori_loop(0, q_ref.shape[1] // kht.shape[0], group, 0)


def hidden_kernel(ids, ctx_own, ctx_other, w_out, emb_own, emb_other, extra0, extra1, slot, h_ref, p_ref, n_ref, send, acc):
    n = emb_own.shape[0]
    half = acc.shape[1]
    k = ids[K]
    mine = pl.ds(pl.multiple_of(k * half, half), half)
    rest = rows_at((1 - k) * half, half)
    acc[rows_at(k * n, n), :] = emb_own[:, mine].astype(F32)
    acc[rows_at((1 - k) * n, n), :] = emb_other[:, mine].astype(F32)
    acc[2 * n :, :] = (extra0[:LEAD, mine] + extra1[:LEAD, mine]).astype(F32)
    mixed = dot(ctx_own[...], w_out[rows_at(k * half, half), mine]) + dot(ctx_other[...], w_out[rest, mine])
    hidden = (acc[...] + mixed).astype(BF16)
    h_ref[...] = hidden[: 2 * n]
    hot = (lax.broadcasted_iota(jnp.int32, (p_ref.shape[0], acc.shape[0]), 0) == slot[...]).astype(F32)
    count = jnp.broadcast_to(jnp.sum(hot, axis=1, keepdims=True), n_ref.shape)
    part = dot(hot.astype(BF16), hidden)
    p_ref[...] = part
    n_ref[...] = count
    send[:, :half] = part.astype(BF16)
    send[:, half:] = count.astype(BF16)


def pool_kernel(ids, part, count, recv, o_ref):
    half = part.shape[1]
    total = part[...] + recv[:, :half].astype(F32)
    number = count[:, :1] + recv[:, half : half + 1].astype(F32)
    o_ref[...] = (total / jnp.maximum(number, 1.0)).astype(BF16)


def up_kernel(ids, half, other, w_own, w_x, w_z, o_ref, pool):
    n = half.shape[1]
    k, c, z = ids[K], ids[C], ids[Z]
    pool[:, pl.ds(pl.multiple_of(k * n, n), n)] = half[...]
    pool[:, pl.ds(pl.multiple_of((1 - k) * n, n), n)] = other[...]
    rows = w_own.shape[0]
    part = rows // 2
    own = dot(pool[:, pl.ds(pl.multiple_of(c * rows, rows), rows)], w_own[...])
    base = (1 - c) * rows
    at_x = pl.multiple_of(base + z * part, part)
    at_z = pl.multiple_of(base + (1 - z) * part, part)
    total = own + dot(pool[:, pl.ds(at_x, part)], w_x[...]) + dot(pool[:, pl.ds(at_z, part)], w_z[...])
    o_ref[...] = total.astype(BF16)


def kv_kernel(ids, totals, l0, l1, l2, l3, gain, wk, wv, w_x, w_z, s_ref, scale_ref, kv_ref):
    n = l0.shape[1]
    t = ids[A] * 2 + ids[K]
    step = 32

    def rows_step(i, _):
        rows = pl.ds(pl.multiple_of(i * step, step), step)
        square = jnp.zeros((step, 1), F32)
        for j, piece in enumerate((l0, l1, l2, l3)):
            at = pl.multiple_of((t ^ j) * n, n)
            floats = piece[rows, :].astype(F32)
            square = square + jnp.sum(floats * floats, axis=-1, keepdims=True)
            s_ref[rows, pl.ds(at, n)] = (floats * gain[:, pl.ds(at, n)]).astype(BF16)
        scale_ref[rows, :] = jnp.broadcast_to(lax.rsqrt(square / (4 * n) + EPS), (step, scale_ref.shape[1]))
        return 0

    lax.fori_loop(0, l0.shape[0] // step, rows_step, 0)
    scale = scale_ref[:, :1]
    rows = wk.shape[0]
    c, z = ids[C], ids[Z]
    mine = s_ref[:, pl.ds(pl.multiple_of(c * rows, rows), rows)]
    base = (1 - c) * rows
    rest = s_ref[:, rows_at(base, rows)]
    slots = l0.shape[0]
    w = wk.shape[1]
    for parity, key, value in ((0, w_x, w_z), (1, w_z, w_x)):

        @pl.when(z == parity)
        def _(key=key, value=value):
            kv_ref[:slots, :w] = ((dot(mine, wk[...]) + dot(rest, key[...])) * scale).astype(BF16)
            kv_ref[:slots, w:] = ((dot(mine, wv[...]) + dot(rest, value[...])) * scale).astype(BF16)

    count = jnp.zeros((kv_ref.shape[0] - slots, 2 * w), F32) + totals[USED].astype(F32)
    kv_ref[slots:, :] = count.astype(BF16)


def q_kernel(ids, s_ref, scale, w_own, x0, z0, x1, z1, q_ref):
    rows = w_own.shape[0]
    part = rows // 2
    w = x0.shape[1]
    c, z = ids[C], ids[Z]
    base = (1 - c) * rows
    mine = s_ref[:, pl.ds(pl.multiple_of(c * rows, rows), rows)]
    sx = s_ref[:, pl.ds(pl.multiple_of(base + z * part, part), part)]
    sz = s_ref[:, pl.ds(pl.multiple_of(base + (1 - z) * part, part), part)]
    for j, (wx, wz) in enumerate(((x0, z0), (x1, z1))):
        total = dot(mine, w_own[:, j * w : (j + 1) * w]) + dot(sx, wx[...]) + dot(sz, wz[...])
        q_ref[:, j * w : (j + 1) * w] = (total * scale[:, :1]).astype(BF16)


def latent_attend(ids, totals, q_ref, kv_own, kv_other, attn):
    slots = q_ref.shape[0]
    d = HEAD_SIZE
    blk = 128
    scale = 1.0 / HEAD_SIZE**0.5
    col = lax.broadcasted_iota(jnp.int32, (blk, slots), 1)
    row = lax.broadcasted_iota(jnp.int32, (blk, slots), 0)
    used_other = kv_other[slots:, :][:1, :1].astype(F32)
    ok_other = col.astype(F32) < jnp.where(ids[C] == 1, used_other, 0.0)
    ones = jnp.ones((slots, d), BF16)
    v_own = jnp.concatenate([kv_own[:slots, d:], ones], axis=1)
    v_other = jnp.concatenate([kv_other[:slots, d:], ones], axis=1)
    for b in range(slots // blk):
        ok_own = (col <= row + b * blk) & (col < totals[USED])
        for h in range(q_ref.shape[1] // d):
            qh = q_ref[b * blk : (b + 1) * blk, h * d : (h + 1) * d]
            s0 = jnp.where(ok_own, dot_nt(qh, kv_own[:slots, :d]) * scale, NEG)
            s1 = jnp.where(ok_other, dot_nt(qh, kv_other[:slots, :d]) * scale, NEG)
            peak = jnp.maximum(jnp.max(s0, axis=-1, keepdims=True), jnp.max(s1, axis=-1, keepdims=True))
            e0 = jnp.exp(s0 - peak).astype(BF16)
            e1 = jnp.exp(s1 - peak).astype(BF16)
            mixed = dot(e0, v_own) + dot(e1, v_other)
            attn[b * blk : (b + 1) * blk, h * d : (h + 1) * d] = (mixed[:, :d] / mixed[:, d:]).astype(BF16)


def project(ids, attn, w_own, x0, z0, pieces, chip, send, keep):
    w = x0.shape[1]
    part = x0.shape[0]
    k, c, z = ids[K], ids[C], ids[Z]

    def store(j, value):
        @pl.when(k == j)
        def _():
            keep[...] = value.astype(keep.dtype)

        @pl.when(k != j)
        def _():
            send[...] = value.astype(send.dtype)

    @pl.when(chip == c)
    def _():
        for j in range(2):
            store(j, dot(attn[...], w_own[:, j * w : (j + 1) * w]))

    @pl.when(chip != c)
    def _():
        at_x, at_z = z * part, (1 - z) * part
        store(0, dot(attn[:, rows_at(at_x, part)], x0[...]) + dot(attn[:, rows_at(at_z, part)], z0[...]))
        n = part // 2
        total = 0.0
        for at, piece in zip((at_x, at_x + n, at_z + n, at_z), pieces):
            total = total + dot(attn[:, rows_at(at, n)], piece[...])
        store(1, total)


def out_far_kernel(ids, totals, q_ref, kv_own, kv_other, w_own, x0, z0, x1, x2, x3, z1, send, keep, attn):
    latent_attend(ids, totals, q_ref, kv_own, kv_other, attn)
    project(ids, attn, w_own, x0, z0, (x1, x2, x3, z1), 1 - ids[A], send, keep)


def out_near_kernel(ids, attn, w_own, x0, z0, x1, x2, x3, z1, send, keep):
    project(ids, attn, w_own, x0, z0, (x1, x2, x3, z1), ids[A], send, keep)


def far_kernel(ids, keep, recv, o_ref):
    o_ref[...] = (keep[...] + recv[...].astype(F32)).astype(BF16)


def down_kernel(ids, latent, near_keep, near_recv, far_recv, w_own, w_x, w_z, send, keep, lo):
    k, c, z = ids[K], ids[C], ids[Z]
    near = latent[...].astype(F32) + near_keep[...] + near_recv[...].astype(F32)
    lo[...] = (near + far_recv[...].astype(F32)).astype(BF16)
    part = w_x.shape[0]
    own = dot(lo[...], w_own[...])
    rest = dot(lo[:, rows_at(z * part, part)], w_x[...]) + dot(lo[:, rows_at((1 - z) * part, part)], w_z[...])

    @pl.when(c == k)
    def _():
        keep[...] = own
        send[...] = rest.astype(BF16)

    @pl.when(c != k)
    def _():
        keep[...] = rest
        send[...] = own.astype(BF16)


def sum_kernel(ids, totals, keep, recv, full, low, trailing):
    full[...] = keep[...] + recv[...].astype(F32)
    low[...] = full[...].astype(BF16)
    trailing[...] = full[pl.ds(totals[LAST], 1), :].astype(BF16)


def final_kernel(ids, hidden, patch, recv, slot, carry0, carry1, kept, send, states):
    patch_out = (patch[...] + recv[...].astype(F32)).astype(BF16)
    rows = hidden.shape[0]
    n = rows // 2
    hot = lax.broadcasted_iota(jnp.int32, (rows, patch.shape[0]), 1) == slot[...]
    spread = dot(hot.astype(F32).astype(BF16), patch_out)
    carried = (carry0[...].astype(F32) + carry1[...].astype(F32)).astype(BF16).astype(F32)
    lead = (slot[...] < 0).astype(F32)
    states[...] = (hidden[...].astype(F32) + spread + lead * carried).astype(BF16)
    k = ids[K]
    kept[...] = states[rows_at(k * n, n), :]
    send[...] = states[rows_at((1 - k) * n, n), :]


def shape(dims, dtype=BF16):
    return jax.ShapeDtypeStruct(dims, dtype)


def local(
    byte_embed,
    patch_start,
    enc_gain,
    enc_qkv,
    enc_out,
    up_proj,
    lat_gain,
    query_proj,
    key_proj,
    value_matrix,
    out_proj,
    down_proj,
):
    nbytes, width = byte_embed.shape
    n_tp = lax.axis_size("tp")
    n_ctx = lax.axis_size("ctx")
    n_dp = lax.axis_size("dp")
    half = width // 2
    slots = n_tp * nbytes // 4
    t = lax.axis_index("tp")
    c = lax.axis_index("ctx")
    zp = lax.axis_index("dp") % 2
    a, k = t // 2, t % 2
    where_k = lambda first, second: jnp.where(k == 0, first, second)

    def swap(x):
        return lax.ppermute(x, "tp", [(i, i ^ 1) for i in range(n_tp)])

    def cross(x):
        return lax.ppermute(x, "tp", [(i, i ^ 2) for i in range(n_tp)])

    def forward(x):
        n = n_ctx * n_tp
        return lax.ppermute(x, ("ctx", "tp"), [(i, i + 2) for i in range(n - 2)])

    def flip(x):
        return lax.ppermute(x, "ctx", [(0, 1), (1, 0)])

    def pair(x):
        return lax.ppermute(x, "dp", [(i, i ^ 1) for i in range(n_dp)])

    paired = n_ctx == 2

    emb_halo = forward(byte_embed)
    emb_other = swap(byte_embed)
    emb_halo_other = swap(emb_halo)

    starts = patch_start.astype(BF16)
    lane = 128
    note = jnp.concatenate([starts[:lane], jnp.ones((width - lane,), BF16)])
    head = jnp.concatenate([byte_embed[:LEAD], jnp.broadcast_to(note[None, :], (16, width))], axis=0)
    extras = []
    for j in range(2):
        extras.append(
            lax.ppermute(head, ("ctx", "tp"), [(g * n_tp, g * n_tp - 2 + j) for g in range(1, n_ctx)])
        )

    one = lambda x: x.astype(jnp.int32)
    place = jnp.stack([one(k), one(a), one(c), one(zp), one(c * 2 + a > 0)])

    starts = starts.reshape(1, nbytes)
    chip_starts = call(join_kernel, place, (starts, swap(starts)), (None,) * 2, [shape((1, 2 * nbytes))])[0]
    chip_far = cross(chip_starts)
    slot_row, slot_col, totals = call(
        meta_kernel,
        place,
        (chip_starts, chip_far, *extras),
        (None,) * 4,
        [shape((1, 2 * nbytes + LEAD), jnp.int32), shape((2 * nbytes, 1), jnp.int32), shape((2,), jnp.int32)],
        [pl.BlockSpec(memory_space=pltpu.VMEM)] * 2 + [SMEM_SPEC],
    )

    if paired:
        rows = lambda w: w.shape[0] // 2
        part = lambda w: pl.BlockSpec((rows(w), w.shape[1]), lambda p, ids: (ids[Z], 0))
        q_cols, o_cols = query_proj.shape[1] // 2, out_proj.shape[1] // 2
        q_rows, o_rows = rows(query_proj), rows(out_proj)
        sizes = [
            *[(q_rows, q_cols)] * 2,
            (o_rows, o_cols),
            *[(o_rows // 2, o_cols)] * 3,
            (rows(down_proj), down_proj.shape[1]),
        ]

        o_rest = pl.BlockSpec((o_rows // 2, o_cols), lambda p, ids: (2 * (1 - ids[Z]) + 1, 1))
        pieces = [
            jnp.where(zp == 0, key_proj, value_matrix),
            lax.dynamic_slice_in_dim(up_proj, zp * rows(up_proj), rows(up_proj), 0),
        ]
        pieces += call(
            halves_kernel,
            place,
            (query_proj, out_proj, out_proj, down_proj),
            [part(query_proj), part(out_proj), o_rest, part(down_proj)],
            [shape(d) for d in sizes],
            [pl.BlockSpec(d, lambda p, ids: (0, 0)) for d in sizes],
            cost=(1e6, 5e6),
        )
        from_x = [flip(p) for p in pieces]
        from_z = [pair(p) if i not in (6, 7) else None for i, p in enumerate(from_x)]

    gain = enc_gain.reshape(1, width)
    n_rows = 2 * nbytes + LEAD
    q, kt, kx, v, wk, wv = call(
        qkv_kernel,
        place,
        (byte_embed, emb_other, *extras, gain, enc_qkv),
        (None, None, None, None, None, pl.BlockSpec(memory_space=pltpu.HBM)),
        [
            shape((n_rows, half)),
            shape((half, 2 * nbytes)),
            shape((LEAD, half)),
            shape((n_rows, half)),
            shape((width, half)),
            shape((width, half)),
        ],
        scratch=[
            pltpu.VMEM((n_rows, width), BF16),
            pltpu.VMEM((width, half), BF16),
            pltpu.SemaphoreType.DMA((3,)),
        ],
        cost=(2 * n_rows * width * 3 * half, 3e6),
    )
    context = call(
        window_kernel,
        place,
        (emb_halo, emb_halo_other, gain, wk, wv, q, kt, kx, v),
        (None,) * 9,
        [shape((n_rows, half))],
        scratch=[
            pltpu.VMEM((2 * nbytes, width), BF16),
            pltpu.VMEM((256, 2 * nbytes), BF16),
            pltpu.VMEM((2 * nbytes, 256), BF16),
        ],
        cost=(8e9, 6e6),
    )[0]
    context_other = swap(context)
    hidden, part_sum, part_count, part_send = call(
        hidden_kernel,
        place,
        (context, context_other, enc_out, byte_embed, emb_other, *extras, slot_row),
        (None,) * 8,
        [
            shape((2 * nbytes, half)),
            shape((slots, half), F32),
            shape((slots, 128), F32),
            shape((slots, half + 128)),
        ],
        scratch=[pltpu.VMEM((n_rows, half), F32)],
        cost=(1.5e9, 4e6),
    )

    part_recv = cross(part_send)
    pooled = call(pool_kernel, place, (part_sum, part_count, part_recv), (None,) * 3, [shape((slots, half))])[0]
    pooled_other = swap(pooled)

    out_cols = out_proj.shape[1] * n_ctx // n_tp
    lat_cols = up_proj.shape[1]
    if paired:
        latent = call(
            up_kernel,
            place,
            (pooled, pooled_other, up_proj, from_x[1], from_z[1]),
            (None,) * 5,
            [shape((slots, lat_cols))],
            scratch=[pltpu.VMEM((slots, width), BF16)],
            cost=(0.6e9, 4e6),
        )[0]
    else:
        whole = where_k(
            jnp.concatenate([pooled, pooled_other], axis=1), jnp.concatenate([pooled_other, pooled], axis=1)
        )
        latent = dot(whole, lax.all_gather(up_proj, "ctx", axis=0, tiled=True)).astype(BF16)

    l2 = cross(latent)
    l1 = swap(latent)
    l3 = swap(l2)
    heads = query_proj.shape[1] // HEAD_SIZE
    kv_w = key_proj.shape[1]
    if paired:
        scaled, scale, kv = call(
            kv_kernel,
            place,
            (totals, latent, l1, l2, l3, lat_gain.reshape(1, -1), key_proj, value_matrix, from_x[0], from_z[0]),
            (SMEM_SPEC, *(None,) * 9),
            [shape((slots, 4 * lat_cols)), shape((slots, 128), F32), shape((slots + 16, 2 * kv_w))],
            cost=(1e9, 6e6),
        )
        kv_far = flip(kv)
        query = call(
            q_kernel,
            place,
            (scaled, scale, query_proj, from_x[2], from_z[2], from_x[3], from_z[3]),
            (None,) * 7,
            [shape((slots, heads * HEAD_SIZE))],
            cost=(1.2e9, 6e6),
        )[0]
        o_weights = (out_proj, from_x[4], from_z[4], from_x[5], from_x[6], from_x[7], from_z[5])
        far_send, far_keep, attn = call(
            out_far_kernel,
            place,
            (totals, query, kv, kv_far, *o_weights),
            (SMEM_SPEC, *(None,) * 10),
            [shape((slots, out_cols)), shape((slots, out_cols), F32), shape((slots, heads * HEAD_SIZE))],
            cost=(1e9, 3e6),
        )
        near_send, near_keep = call(
            out_near_kernel,
            place,
            (attn, *o_weights),
            (None,) * 8,
            [shape((slots, out_cols)), shape((slots, out_cols), F32)],
            cost=(1e9, 3e6),
        )
    else:
        stacked = jnp.stack([latent, l1, l2, l3])
        lat = jnp.concatenate(
            [lax.dynamic_index_in_dim(stacked, t ^ i, 0, keepdims=False) for i in range(n_tp)], axis=1
        )
        lnorm = normed_rows(lat, lat_gain)
        used = lax.all_gather(totals[:1], "ctx", axis=0, tiled=True)
        rows_iota = jnp.arange(slots, dtype=jnp.int32)
        gather = lambda w, axis: lax.all_gather(w, "ctx", axis=axis, tiled=True)
        query = dot(lnorm, gather(query_proj, 0)).astype(BF16)
        kv = jnp.concatenate([dot(lnorm, gather(key_proj, 0)), dot(lnorm, gather(value_matrix, 0))], axis=1)
        keys = gather(kv.astype(BF16), 0)
        key_rows = jnp.arange(keys.shape[0], dtype=jnp.int32)
        allowed = (key_rows % slots < used[key_rows // slots])[None, :] & (
            key_rows[None, :] <= (c * slots + rows_iota)[:, None]
        )
        qh = jnp.transpose(query.reshape(slots, heads, HEAD_SIZE), (1, 0, 2))
        scores = jnp.einsum("hqd,kd->hqk", qh, keys[:, :kv_w], preferred_element_type=F32) / HEAD_SIZE**0.5
        scores = jnp.where(allowed[None], scores, NEG)
        expo = jnp.where(allowed[None], jnp.exp(scores - jnp.max(scores, axis=-1, keepdims=True)), 0.0)
        total = jnp.sum(expo, axis=-1, keepdims=True)
        mixed = jnp.einsum("hqk,kd->hqd", expo.astype(BF16), keys[:, kv_w:], preferred_element_type=F32) / total
        attn = jnp.transpose(mixed, (1, 0, 2)).reshape(slots, heads * HEAD_SIZE).astype(BF16)
        full = dot(attn, gather(out_proj, 1))
        pick = lambda j: lax.dynamic_slice_in_dim(full, (t ^ j) * out_cols, out_cols, 1)
        near_keep, near_send, far_keep, far_send = pick(0), pick(1).astype(BF16), pick(2), pick(3).astype(BF16)

    far = call(far_kernel, place, (far_keep, swap(far_send)), (None,) * 2, [shape((slots, out_cols))])[0]
    far_recv = cross(far)
    near_recv = swap(near_send)
    if paired:
        down_send, down_keep = call(
            down_kernel,
            place,
            (latent, near_keep, near_recv, far_recv, down_proj, from_x[8], from_z[8]),
            (None,) * 7,
            [shape((slots, half)), shape((slots, half), F32)],
            scratch=[pltpu.VMEM((slots, lat_cols), BF16)],
            cost=(0.6e9, 4e6),
        )
    else:
        base = latent.astype(F32) + near_keep + near_recv.astype(F32)
        latent_out = (base + far_recv.astype(F32)).astype(BF16)
        full = dot(latent_out, gather(down_proj, 1))
        down_keep = lax.dynamic_slice_in_dim(full, k * half, half, 1)
        down_send = lax.dynamic_slice_in_dim(full, (1 - k) * half, half, 1).astype(BF16)

    chip_sum, chip_low, trailing = call(
        sum_kernel,
        place,
        (totals, down_keep, swap(down_send)),
        (SMEM_SPEC, None, None),
        [shape((slots, half), F32), shape((slots, half)), shape((1, half))],
    )
    sum_recv = cross(chip_low)
    ahead = lambda at: [(g * n_tp + at * 2 + j, (g + 1) * n_tp + j) for g in range(n_ctx - 1) for j in range(2)]
    carry0 = lax.ppermute(trailing, ("ctx", "tp"), ahead(0))
    carry1 = lax.ppermute(trailing, ("ctx", "tp"), ahead(1))
    kept, send = call(
        final_kernel,
        place,
        (hidden, chip_sum, sum_recv, slot_col, carry0, carry1),
        (None,) * 6,
        [shape((nbytes, half))] * 2,
        scratch=[pltpu.VMEM((2 * nbytes, half), BF16)],
        cost=(0.4e9, 3e6),
    )
    got = swap(send)
    return where_k(jnp.concatenate([kept, got], axis=1), jnp.concatenate([got, kept], axis=1))


def solution(mesh):
    placed = (
        P(("dp", "ctx", "tp"), None),
        P(("dp", "ctx", "tp")),
        P(),
        P(),
        P(),
        P("ctx", "tp"),
        P(),
        P("ctx", "tp"),
        P("ctx", "tp"),
        P("ctx", "tp"),
        P("tp", "ctx"),
        P("tp", "ctx"),
    )

    return jax.shard_map(local, mesh=mesh, in_specs=placed, out_specs=P(("dp", "ctx", "tp"), None), check_vma=False)
```

```python
import functools

import jax
import jax.numpy as jnp
from jax import lax
from jax.experimental import pallas as pl
from jax.experimental.pallas import tpu as pltpu
from jax.sharding import PartitionSpec as P


HB = 64
HEAD_SIZE = 128
EPS = 1e-05
LEAD = 32
NEG = -1e30
VMEM_LIMIT = 24 << 20
F32 = jnp.float32
BF16 = jnp.bfloat16


def dot(a, b):
    return jnp.dot(a, b, preferred_element_type=F32)


def dot_nt(a, b):
    return lax.dot_general(a, b, (((1,), (1,)), ((), ())), preferred_element_type=F32)


def normed_rows(x, gain):
    floats = x.astype(F32)
    scale = lax.rsqrt(jnp.mean(floats * floats, axis=-1, keepdims=True) + EPS)
    return (floats * scale * gain).astype(BF16)


def call(body, ids, args, in_specs, outs, out_specs=None, grid=(1,), scratch=(), cost=(1e7, 1e6), limit=VMEM_LIMIT):
    whole = pl.BlockSpec(memory_space=pltpu.VMEM)
    flops, nbytes = cost
    return pl.pallas_call(
        body,
        out_shape=outs,
        grid_spec=pltpu.PrefetchScalarGridSpec(
            num_scalar_prefetch=1,
            grid=grid,
            in_specs=[whole if spec is None else spec for spec in in_specs],
            out_specs=[whole] * len(outs) if out_specs is None else out_specs,
            scratch_shapes=list(scratch),
        ),
        compiler_params=pltpu.CompilerParams(
            dimension_semantics=("arbitrary",) * len(grid), vmem_limit_bytes=limit
        ),
        cost_estimate=pl.CostEstimate(flops=int(flops), bytes_accessed=int(nbytes), transcendentals=0),
    )(ids, *args)


K, A, C, Z, PREV = range(5)
USED, LAST = range(2)
SMEM_SPEC = pl.BlockSpec(memory_space=pltpu.SMEM)


def rows_at(start, n):
    return pl.ds(pl.multiple_of(start, n), n)


def first_kernel(ids, emb, starts, key, value, up, head, starts_out, kv_out, up_out):
    n, lane = LEAD, 128
    floats = starts[...].astype(F32)
    starts_out[...] = floats.astype(BF16)
    head[:n, :] = emb[...]
    head[n:, :] = jnp.ones((head.shape[0] - n, head.shape[1]), BF16)
    head[n:, :lane] = jnp.broadcast_to(floats[:, :lane], (head.shape[0] - n, lane)).astype(BF16)
    up_out[...] = up[...]

    @pl.when(ids[Z] == 0)
    def _():
        kv_out[...] = key[...]

    @pl.when(ids[Z] != 0)
    def _():
        kv_out[...] = value[...]


def halves_kernel(ids, query, out, out_rest, down, q0, q1, o0, o1, o2, o3, d0, d1):
    w = q0.shape[1]
    q0[...] = query[:, :w]
    q1[...] = query[:, w:]
    w = o0.shape[1]
    n = o1.shape[0]
    o0[...] = out[:, :w]
    o1[...] = out[:n, w:]
    o2[...] = out[n:, w:]
    o3[...] = out_rest[...]
    n = d0.shape[0]
    d0[...] = down[:n]
    d1[...] = down[n:]


def join_kernel(ids, own, other, o_ref):
    n = own.shape[1]
    k = ids[K]
    o_ref[:, rows_at(k * n, n)] = own[...]
    o_ref[:, rows_at((1 - k) * n, n)] = other[...]


def meta_kernel(ids, mine, other, extra0, extra1, slot_row, slot_col, totals):
    n = mine.shape[1]
    a = ids[A]
    lane = 128
    upper = (
        lax.broadcasted_iota(jnp.int32, (lane, lane), 0) <= lax.broadcasted_iota(jnp.int32, (lane, lane), 1)
    ).astype(F32).astype(BF16)

    def prefix(starts):
        return dot(jnp.broadcast_to(starts, (8, lane)).astype(BF16), upper)[:1]

    row_mine, row_other = mine[...].astype(F32), other[...].astype(F32)
    total_mine, total_other = jnp.sum(row_mine), jnp.sum(row_other)
    base = jnp.zeros((1, 1), F32) + jnp.where(a == 1, total_other, 0.0)
    for j in range(n // lane):
        at = slice(j * lane, (j + 1) * lane)
        sums = prefix(row_mine[:, at]) + base
        slot_row[:, at] = sums.astype(jnp.int32) - 1
        base = sums[:, lane - 1 :]
    own_used = (total_mine + total_other).astype(jnp.int32)
    follow = (extra0[LEAD:, :] + extra1[LEAD:, :])[:1].astype(F32)
    led = prefix(follow[:, :lane])[:, :LEAD]
    leads = (led < 0.5) & (follow[:, lane : lane + 1] > 0.5)
    slot_row[:, n:] = jnp.where(leads, own_used - 1, -1)
    row = lax.broadcasted_iota(jnp.int32, (n, n), 0)
    col = lax.broadcasted_iota(jnp.int32, (n, n), 1)
    slot_col[...] = jnp.sum(jnp.where(row == col, slot_row[:, :n].astype(F32), 0.0), axis=1, keepdims=True).astype(
        jnp.int32
    )
    totals[USED] = own_used
    totals[LAST] = own_used - 1


def qkv_kernel(ids, own, other, extra0, extra1, gain, w_hbm, q_ref, kt_ref, kx_ref, v_ref, wk, wv, normed, wq, sems):
    n, width = own.shape
    half = width // 2
    k = ids[K]
    copies = []
    for part, target in ((1, wk), (2, wv), (0, wq)):
        at = pl.ds(pl.multiple_of(part * width + k * half, half), half)
        copies.append(pltpu.make_async_copy(w_hbm.at[:, at], target, sems.at[part]))
        copies[-1].start()
    normed[rows_at(k * n, n), :] = normed_rows(own[...], gain[...])
    normed[rows_at((1 - k) * n, n), :] = normed_rows(other[...], gain[...])
    normed[2 * n :, :] = normed_rows(extra0[:LEAD, :] + extra1[:LEAD, :], gain[...])
    for copy in copies:
        copy.wait()
    w = 256
    for j in range(half // w):
        at = slice(j * w, (j + 1) * w)
        keys = dot(normed[...], wk[:, at])
        kx_ref[:, at] = keys[2 * n :].astype(BF16)
        kt_ref[at, :] = jnp.transpose(keys[: 2 * n]).astype(BF16)
        v_ref[:, at] = dot(normed[...], wv[:, at]).astype(BF16)
        q_ref[:, at] = (dot(normed[...], wq[:, at]).astype(BF16).astype(F32) * (1.0 / HB**0.5)).astype(BF16)


def halo_kernel(ids, own, other, gain, normed):
    n = own.shape[0]
    k = ids[K]
    normed[rows_at(k * n, n), :] = normed_rows(own[...], gain[...])
    normed[rows_at((1 - k) * n, n), :] = normed_rows(other[...], gain[...])


def window_kernel(ids, normed, wk, wv, q_ref, kt_ref, kx_ref, v_ref, o_ref, kht, vh, *, g):
    n = normed.shape[0] // 2
    rows = 2 * n
    n_extra = q_ref.shape[0] - rows
    blk = 128
    lanes = 2 * HB
    nblk = rows // blk
    bias = jnp.where(ids[PREV] == 1, 0.0, NEG).astype(F32)
    low = lax.broadcasted_iota(jnp.int32, (blk, lanes), 1) < HB
    r = lax.broadcasted_iota(jnp.int32, (2 * blk, blk), 0)
    causal = lax.broadcasted_iota(jnp.int32, (2 * blk, blk), 1) <= jnp.where(r >= blk, r - blk, r)
    re = lax.broadcasted_iota(jnp.int32, (2 * n_extra, rows), 0)
    re = jnp.where(re >= n_extra, re - n_extra, re)
    ok_own = lax.broadcasted_iota(jnp.int32, (2 * n_extra, rows), 1) > re
    ok_new = lax.broadcasted_iota(jnp.int32, (2 * n_extra, n_extra), 1) <= re[:, :n_extra]

    def split(qb):
        keep = low[: qb.shape[0]]
        none = jnp.zeros_like(qb)
        return jnp.concatenate([jnp.where(keep, qb, none), jnp.where(keep, none, qb)], axis=0)

    def join(mixed):
        m = mixed.shape[0] // 2
        mixed = mixed[:, :lanes] / mixed[:, lanes:]
        return jnp.where(low[:m], mixed[:m], mixed[m:]).astype(BF16)

    def weighted(e, v):
        return dot(e.astype(BF16), jnp.concatenate([v, jnp.ones_like(v)], axis=1))

    w = kht.shape[0]
    wide = slice(g * w, (g + 1) * w)
    kht[...] = jnp.transpose(dot(normed[...], wk[:, wide])).astype(BF16)
    vh[...] = dot(normed[...], wv[:, wide]).astype(BF16)
    for pair in range(w // lanes):
        cols = slice(g * w + pair * lanes, g * w + (pair + 1) * lanes)
        part = slice(pair * lanes, (pair + 1) * lanes)
        for b in range(nblk):
            q2 = split(q_ref[b * blk : (b + 1) * blk, cols])
            s_own = dot(q2, kt_ref[cols, : (b + 1) * blk])
            s_halo = dot(q2, kht[part, b * blk :]) + bias
            diag = jnp.where(causal, s_own[:, b * blk :], s_halo[:, :blk])
            peak = jnp.max(diag, axis=-1, keepdims=True)
            if b > 0:
                peak = jnp.maximum(peak, jnp.max(s_own[:, : b * blk], axis=-1, keepdims=True))
            if b < nblk - 1:
                peak = jnp.maximum(peak, jnp.max(s_halo[:, blk:], axis=-1, keepdims=True))
            e_diag = jnp.exp(diag - peak)
            e_own = jnp.where(causal, e_diag, 0.0)
            e_halo = jnp.where(causal, 0.0, e_diag)
            if b > 0:
                e_own = jnp.concatenate([jnp.exp(s_own[:, : b * blk] - peak), e_own], axis=1)
            if b < nblk - 1:
                e_halo = jnp.concatenate([e_halo, jnp.exp(s_halo[:, blk:] - peak)], axis=1)
            mixed = weighted(e_own, v_ref[: (b + 1) * blk, cols]) + weighted(e_halo, vh[b * blk :, part])
            o_ref[b * blk : (b + 1) * blk, part] = join(mixed)
        q2 = split(q_ref[rows:, cols])
        s_own = jnp.where(ok_own, dot(q2, kt_ref[cols, :]), NEG)
        s_new = jnp.where(ok_new, dot_nt(q2, kx_ref[:, cols]), NEG)
        peak = jnp.maximum(jnp.max(s_own, axis=-1, keepdims=True), jnp.max(s_new, axis=-1, keepdims=True))
        mixed = weighted(jnp.exp(s_own - peak), v_ref[:rows, cols]) + weighted(
            jnp.exp(s_new - peak), v_ref[rows:, cols]
        )
        o_ref[rows:, part] = join(mixed)


def hidden_kernel(ids, own0, own1, other0, other1, w_out, emb_own, emb_other, extra0, extra1, slot, h_ref, p_ref, n_ref, send, acc):
    n = emb_own.shape[0]
    half = acc.shape[1]
    k = ids[K]
    mine = pl.ds(pl.multiple_of(k * half, half), half)
    acc[rows_at(k * n, n), :] = emb_own[:, mine].astype(F32)
    acc[rows_at((1 - k) * n, n), :] = emb_other[:, mine].astype(F32)
    acc[2 * n :, :] = (extra0[:LEAD, mine] + extra1[:LEAD, mine]).astype(F32)
    w = own0.shape[1]
    mixed = 0.0
    for at, shift, piece in ((k, 0, own0), (k, w, own1), (1 - k, 0, other0), (1 - k, w, other1)):
        mixed = mixed + dot(piece[...], w_out[rows_at(at * half + shift, w), mine])
    hidden = (acc[...] + mixed).astype(BF16)
    h_ref[...] = hidden[: 2 * n]
    hot = (lax.broadcasted_iota(jnp.int32, (p_ref.shape[0], acc.shape[0]), 0) == slot[...]).astype(F32)
    count = jnp.broadcast_to(jnp.sum(hot, axis=1, keepdims=True), n_ref.shape)
    part = dot(hot.astype(BF16), hidden)
    p_ref[...] = part
    n_ref[...] = count
    send[:, :half] = part.astype(BF16)
    send[:, half:] = count.astype(BF16)


def pool_kernel(ids, part, count, recv, o_ref):
    half = part.shape[1]
    total = part[...] + recv[:, :half].astype(F32)
    number = count[:, :1] + recv[:, half : half + 1].astype(F32)
    o_ref[...] = (total / jnp.maximum(number, 1.0)).astype(BF16)


def up_kernel(ids, half, other, w_own, w_x, w_z, o_ref, pool):
    n = half.shape[1]
    k, c, z = ids[K], ids[C], ids[Z]
    pool[:, pl.ds(pl.multiple_of(k * n, n), n)] = half[...]
    pool[:, pl.ds(pl.multiple_of((1 - k) * n, n), n)] = other[...]
    rows = w_own.shape[0]
    part = rows // 2
    own = dot(pool[:, pl.ds(pl.multiple_of(c * rows, rows), rows)], w_own[...])
    base = (1 - c) * rows
    at_x = pl.multiple_of(base + z * part, part)
    at_z = pl.multiple_of(base + (1 - z) * part, part)
    total = own + dot(pool[:, pl.ds(at_x, part)], w_x[...]) + dot(pool[:, pl.ds(at_z, part)], w_z[...])
    o_ref[...] = total.astype(BF16)


def kv_kernel(ids, totals, l0, l1, l2, l3, gain, wk, wv, w_x, w_z, s_ref, scale_ref, kv_ref):
    n = l0.shape[1]
    t = ids[A] * 2 + ids[K]
    step = 32

    def rows_step(i, _):
        rows = pl.ds(pl.multiple_of(i * step, step), step)
        square = jnp.zeros((step, 1), F32)
        for j, piece in enumerate((l0, l1, l2, l3)):
            at = pl.multiple_of((t ^ j) * n, n)
            floats = piece[rows, :].astype(F32)
            square = square + jnp.sum(floats * floats, axis=-1, keepdims=True)
            s_ref[rows, pl.ds(at, n)] = (floats * gain[:, pl.ds(at, n)]).astype(BF16)
        scale_ref[rows, :] = jnp.broadcast_to(lax.rsqrt(square / (4 * n) + EPS), (step, scale_ref.shape[1]))
        return 0

    lax.fori_loop(0, l0.shape[0] // step, rows_step, 0)
    scale = scale_ref[:, :1]
    rows = wk.shape[0]
    c, z = ids[C], ids[Z]
    mine = s_ref[:, pl.ds(pl.multiple_of(c * rows, rows), rows)]
    base = (1 - c) * rows
    rest = s_ref[:, rows_at(base, rows)]
    slots = l0.shape[0]
    w = wk.shape[1]
    for parity, key, value in ((0, w_x, w_z), (1, w_z, w_x)):

        @pl.when(z == parity)
        def _(key=key, value=value):
            kv_ref[:slots, :w] = ((dot(mine, wk[...]) + dot(rest, key[...])) * scale).astype(BF16)
            kv_ref[:slots, w:] = ((dot(mine, wv[...]) + dot(rest, value[...])) * scale).astype(BF16)

    count = jnp.zeros((kv_ref.shape[0] - slots, 2 * w), F32) + totals[USED].astype(F32)
    kv_ref[slots:, :] = count.astype(BF16)


def q_kernel(ids, s_ref, scale, w_own, x0, z0, x1, z1, q_ref):
    rows = w_own.shape[0]
    part = rows // 2
    w = x0.shape[1]
    c, z = ids[C], ids[Z]
    base = (1 - c) * rows
    mine = s_ref[:, pl.ds(pl.multiple_of(c * rows, rows), rows)]
    sx = s_ref[:, pl.ds(pl.multiple_of(base + z * part, part), part)]
    sz = s_ref[:, pl.ds(pl.multiple_of(base + (1 - z) * part, part), part)]
    for j, (wx, wz) in enumerate(((x0, z0), (x1, z1))):
        total = dot(mine, w_own[:, j * w : (j + 1) * w]) + dot(sx, wx[...]) + dot(sz, wz[...])
        q_ref[:, j * w : (j + 1) * w] = (total * scale[:, :1]).astype(BF16)


def latent_attend(ids, totals, q_ref, kv_own, kv_other, attn):
    slots = q_ref.shape[0]
    d = HEAD_SIZE
    blk = 128
    scale = 1.0 / HEAD_SIZE**0.5
    col = lax.broadcasted_iota(jnp.int32, (blk, slots), 1)
    row = lax.broadcasted_iota(jnp.int32, (blk, slots), 0)
    used_other = kv_other[slots:, :][:1, :1].astype(F32)
    ok_other = col.astype(F32) < jnp.where(ids[C] == 1, used_other, 0.0)
    ones = jnp.ones((slots, d), BF16)
    v_own = jnp.concatenate([kv_own[:slots, d:], ones], axis=1)
    v_other = jnp.concatenate([kv_other[:slots, d:], ones], axis=1)
    for b in range(slots // blk):
        ok_own = (col <= row + b * blk) & (col < totals[USED])
        for h in range(q_ref.shape[1] // d):
            qh = q_ref[b * blk : (b + 1) * blk, h * d : (h + 1) * d]
            s0 = jnp.where(ok_own, dot_nt(qh, kv_own[:slots, :d]) * scale, NEG)
            s1 = jnp.where(ok_other, dot_nt(qh, kv_other[:slots, :d]) * scale, NEG)
            peak = jnp.maximum(jnp.max(s0, axis=-1, keepdims=True), jnp.max(s1, axis=-1, keepdims=True))
            e0 = jnp.exp(s0 - peak).astype(BF16)
            e1 = jnp.exp(s1 - peak).astype(BF16)
            mixed = dot(e0, v_own) + dot(e1, v_other)
            attn[b * blk : (b + 1) * blk, h * d : (h + 1) * d] = (mixed[:, :d] / mixed[:, d:]).astype(BF16)


def blocks_of(attn, w_own, x0, z0, pieces, chip, c, z, store, which):
    w, part = x0.shape[1], x0.shape[0]

    @pl.when(chip == c)
    def _():
        for j in which:
            store(j, dot(attn[...], w_own[:, j * w : (j + 1) * w]))

    @pl.when(chip != c)
    def _():
        at_x, at_z = z * part, (1 - z) * part
        if 0 in which:
            store(0, dot(attn[:, rows_at(at_x, part)], x0[...]) + dot(attn[:, rows_at(at_z, part)], z0[...]))
        if 1 in which:
            n = part // 2
            total = 0.0
            for at, piece in zip((at_x, at_x + n, at_z + n, at_z), pieces):
                total = total + dot(attn[:, rows_at(at, n)], piece[...])
            store(1, total)


def attend_kernel(ids, totals, q_ref, kv_own, kv_other, attn):
    latent_attend(ids, totals, q_ref, kv_own, kv_other, attn)


def far0_kernel(ids, attn, w_own, x0, z0, full, low):
    def store(j, value):
        full[...] = value
        low[...] = value.astype(BF16)

    blocks_of(attn, w_own, x0, z0, (), 1 - ids[A], ids[C], ids[Z], store, (0,))


def far1_kernel(ids, attn, w_own, x0, x1, x2, x3, z1, full, low):
    def store(j, value):
        full[...] = value
        low[...] = value.astype(BF16)

    blocks_of(attn, w_own, x0, None, (x1, x2, x3, z1), 1 - ids[A], ids[C], ids[Z], store, (1,))


def near_kernel(ids, attn, w_own, x0, z0, x1, x2, x3, z1, send, keep):
    k = ids[K]

    def store(j, value):
        @pl.when(k == j)
        def _():
            keep[...] = value.astype(keep.dtype)

        @pl.when(k != j)
        def _():
            send[...] = value.astype(send.dtype)

    blocks_of(attn, w_own, x0, z0, (x1, x2, x3, z1), ids[A], ids[C], ids[Z], store, (0, 1))


def far_kernel(ids, keep, recv, o_ref):
    o_ref[...] = (keep[...] + recv[...].astype(F32)).astype(BF16)


def down_kernel(ids, latent, near_keep, near_recv, far0, far1, w_own, x0, x1, z0, z1, send, keep, lo):
    k, c, z = ids[K], ids[C], ids[Z]
    near = latent[...].astype(F32) + near_keep[...] + near_recv[...].astype(F32)
    lo[...] = (near + far0[...].astype(F32) + far1[...].astype(F32)).astype(BF16)
    n = x0.shape[0]
    part = 2 * n
    own = dot(lo[...], w_own[...])
    at_x, at_z = z * part, (1 - z) * part
    rest = 0.0
    for at, piece in ((at_x, x0), (at_x + n, x1), (at_z, z0), (at_z + n, z1)):
        rest = rest + dot(lo[:, rows_at(at, n)], piece[...])

    @pl.when(c == k)
    def _():
        keep[...] = own
        send[...] = rest.astype(BF16)

    @pl.when(c != k)
    def _():
        keep[...] = rest
        send[...] = own.astype(BF16)


def sum_kernel(ids, totals, keep, recv, full, low, trailing):
    full[...] = keep[...] + recv[...].astype(F32)
    low[...] = full[...].astype(BF16)
    trailing[...] = full[pl.ds(totals[LAST], 1), :].astype(BF16)


def final_kernel(ids, hidden, patch, recv, slot, carry0, carry1, kept, send, states):
    patch_out = (patch[...] + recv[...].astype(F32)).astype(BF16)
    rows = hidden.shape[0]
    n = rows // 2
    hot = lax.broadcasted_iota(jnp.int32, (rows, patch.shape[0]), 1) == slot[...]
    spread = dot(hot.astype(F32).astype(BF16), patch_out)
    carried = (carry0[...].astype(F32) + carry1[...].astype(F32)).astype(BF16).astype(F32)
    lead = (slot[...] < 0).astype(F32)
    states[...] = (hidden[...].astype(F32) + spread + lead * carried).astype(BF16)
    k = ids[K]
    kept[...] = states[rows_at(k * n, n), :]
    send[...] = states[rows_at((1 - k) * n, n), :]


def shape(dims, dtype=BF16):
    return jax.ShapeDtypeStruct(dims, dtype)


def local(
    byte_embed,
    patch_start,
    enc_gain,
    enc_qkv,
    enc_out,
    up_proj,
    lat_gain,
    query_proj,
    key_proj,
    value_matrix,
    out_proj,
    down_proj,
):
    nbytes, width = byte_embed.shape
    n_tp = lax.axis_size("tp")
    n_ctx = lax.axis_size("ctx")
    n_dp = lax.axis_size("dp")
    half = width // 2
    slots = n_tp * nbytes // 4
    t = lax.axis_index("tp")
    c = lax.axis_index("ctx")
    zp = lax.axis_index("dp") % 2
    a, k = t // 2, t % 2
    where_k = lambda first, second: jnp.where(k == 0, first, second)

    def swap(x):
        return lax.ppermute(x, "tp", [(i, i ^ 1) for i in range(n_tp)])

    def cross(x):
        return lax.ppermute(x, "tp", [(i, i ^ 2) for i in range(n_tp)])

    def forward(x):
        n = n_ctx * n_tp
        return lax.ppermute(x, ("ctx", "tp"), [(i, i + 2) for i in range(n - 2)])

    def flip(x):
        return lax.ppermute(x, "ctx", [(0, 1), (1, 0)])

    def pair(x):
        return lax.ppermute(x, "dp", [(i, i ^ 1) for i in range(n_dp)])

    paired = n_ctx == 2

    emb_halo = forward(byte_embed)
    emb_other = swap(byte_embed)
    emb_halo_other = swap(emb_halo)

    one = lambda x: x.astype(jnp.int32)
    place = jnp.stack([one(k), one(a), one(c), one(zp), one(c * 2 + a > 0)])

    in_hbm = lambda x: pltpu.with_memory_space_constraint(x, pltpu.HBM)

    up_rows = up_proj.shape[0] // 2
    block_of = lambda rows, cols, at: pl.BlockSpec((rows, cols), lambda p, ids: (at(ids), 0))
    origin = lambda ids: 0
    head, starts, kv_piece, up_piece = call(
        first_kernel,
        place,
        (in_hbm(byte_embed), in_hbm(patch_start.reshape(1, nbytes)), in_hbm(key_proj), in_hbm(value_matrix), in_hbm(up_proj)),
        [
            block_of(LEAD, width, origin),
            block_of(1, nbytes, origin),
            block_of(*key_proj.shape, origin),
            block_of(*value_matrix.shape, origin),
            block_of(up_rows, up_proj.shape[1], lambda ids: ids[Z]),
        ],
        [shape((LEAD + 16, width)), shape((1, nbytes)), shape(key_proj.shape), shape((up_rows, up_proj.shape[1]))],
        cost=(1e6, 3e6),
    )
    extras = []
    for j in range(2):
        extras.append(
            lax.ppermute(head, ("ctx", "tp"), [(g * n_tp, g * n_tp - 2 + j) for g in range(1, n_ctx)])
        )

    chip_starts = call(join_kernel, place, (starts, swap(starts)), (None,) * 2, [shape((1, 2 * nbytes))])[0]
    chip_far = cross(chip_starts)
    slot_row, slot_col, totals = call(
        meta_kernel,
        place,
        (chip_starts, chip_far, *extras),
        (None,) * 4,
        [shape((1, 2 * nbytes + LEAD), jnp.int32), shape((2 * nbytes, 1), jnp.int32), shape((2,), jnp.int32)],
        [pl.BlockSpec(memory_space=pltpu.VMEM)] * 2 + [SMEM_SPEC],
    )

    if paired:
        rows = lambda w: w.shape[0] // 2
        part = lambda w: pl.BlockSpec((rows(w), w.shape[1]), lambda p, ids: (ids[Z], 0))
        q_cols, o_cols = query_proj.shape[1] // 2, out_proj.shape[1] // 2
        q_rows, o_rows = rows(query_proj), rows(out_proj)
        sizes = [
            *[(q_rows, q_cols)] * 2,
            (o_rows, o_cols),
            *[(o_rows // 2, o_cols)] * 3,
            *[(rows(down_proj) // 2, down_proj.shape[1])] * 2,
        ]

        o_rest = pl.BlockSpec((o_rows // 2, o_cols), lambda p, ids: (2 * (1 - ids[Z]) + 1, 1))
        pieces = [up_piece, kv_piece]
        pieces += call(
            halves_kernel,
            place,
            (query_proj, out_proj, out_proj, down_proj),
            [part(query_proj), part(out_proj), o_rest, part(down_proj)],
            [shape(d) for d in sizes],
            [pl.BlockSpec(d, lambda p, ids: (0, 0)) for d in sizes],
            cost=(1e6, 5e6),
        )
        from_x = [flip(p) for p in pieces]
        from_z = [pair(p) if i not in (6, 7) else None for i, p in enumerate(from_x)]

    gain = enc_gain.reshape(1, width)
    n_rows = 2 * nbytes + LEAD
    q, kt, kx, v, wk, wv = call(
        qkv_kernel,
        place,
        (byte_embed, emb_other, *extras, gain, in_hbm(enc_qkv)),
        (None, None, None, None, None, pl.BlockSpec(memory_space=pltpu.HBM)),
        [
            shape((n_rows, half)),
            shape((half, 2 * nbytes)),
            shape((LEAD, half)),
            shape((n_rows, half)),
            shape((width, half)),
            shape((width, half)),
        ],
        scratch=[
            pltpu.VMEM((n_rows, width), BF16),
            pltpu.VMEM((width, half), BF16),
            pltpu.SemaphoreType.DMA((3,)),
        ],
        cost=(2 * n_rows * width * 3 * half, 3e6),
    )
    normed = call(
        halo_kernel, place, (emb_halo, emb_halo_other, gain), (None,) * 3, [shape((2 * nbytes, width))], cost=(1e7, 2e6)
    )[0]
    context, context_other = [], []
    for g in range(half // 256):
        context.append(
            call(
                functools.partial(window_kernel, g=g),
                place,
                (normed, wk, wv, q, kt, kx, v),
                (None,) * 7,
                [shape((n_rows, 256))],
                scratch=[pltpu.VMEM((256, 2 * nbytes), BF16), pltpu.VMEM((2 * nbytes, 256), BF16)],
                cost=(4e9, 3e6),
            )[0]
        )
        context_other.append(swap(context[-1]))
    hidden, part_sum, part_count, part_send = call(
        hidden_kernel,
        place,
        (*context, *context_other, enc_out, byte_embed, emb_other, *extras, slot_row),
        (None,) * 10,
        [
            shape((2 * nbytes, half)),
            shape((slots, half), F32),
            shape((slots, 128), F32),
            shape((slots, half + 128)),
        ],
        scratch=[pltpu.VMEM((n_rows, half), F32)],
        cost=(1.5e9, 4e6),
    )

    part_recv = cross(part_send)
    pooled = call(pool_kernel, place, (part_sum, part_count, part_recv), (None,) * 3, [shape((slots, half))])[0]
    pooled_other = swap(pooled)

    out_cols = out_proj.shape[1] * n_ctx // n_tp
    lat_cols = up_proj.shape[1]
    if paired:
        latent = call(
            up_kernel,
            place,
            (pooled, pooled_other, up_proj, from_x[0], from_z[0]),
            (None,) * 5,
            [shape((slots, lat_cols))],
            scratch=[pltpu.VMEM((slots, width), BF16)],
            cost=(0.6e9, 4e6),
        )[0]
    else:
        whole = where_k(
            jnp.concatenate([pooled, pooled_other], axis=1), jnp.concatenate([pooled_other, pooled], axis=1)
        )
        latent = dot(whole, lax.all_gather(up_proj, "ctx", axis=0, tiled=True)).astype(BF16)

    l2 = cross(latent)
    l1 = swap(latent)
    l3 = swap(l2)
    heads = query_proj.shape[1] // HEAD_SIZE
    kv_w = key_proj.shape[1]
    if paired:
        scaled, scale, kv = call(
            kv_kernel,
            place,
            (totals, latent, l1, l2, l3, lat_gain.reshape(1, -1), key_proj, value_matrix, from_x[1], from_z[1]),
            (SMEM_SPEC, *(None,) * 9),
            [shape((slots, 4 * lat_cols)), shape((slots, 128), F32), shape((slots + 16, 2 * kv_w))],
            cost=(1e9, 6e6),
        )
        kv_far = flip(kv)
        query = call(
            q_kernel,
            place,
            (scaled, scale, query_proj, from_x[2], from_z[2], from_x[3], from_z[3]),
            (None,) * 7,
            [shape((slots, heads * HEAD_SIZE))],
            cost=(1.2e9, 6e6),
        )[0]
        attn = call(
            attend_kernel,
            place,
            (totals, query, kv, kv_far),
            (SMEM_SPEC, None, None, None),
            [shape((slots, heads * HEAD_SIZE))],
            cost=(5e8, 1e6),
        )[0]
        o1 = (from_x[5], from_x[6], from_x[7], from_z[5])
        block_out = [shape((slots, out_cols), F32), shape((slots, out_cols))]
        far0 = call(far0_kernel, place, (attn, out_proj, from_x[4], from_z[4]), (None,) * 4, block_out, cost=(3e8, 2e6))
        far1 = call(far1_kernel, place, (attn, out_proj, from_x[4], *o1), (None,) * 7, block_out, cost=(3e8, 2e6))
        near_send, near_keep = call(
            near_kernel,
            place,
            (attn, out_proj, from_x[4], from_z[4], *o1),
            (None,) * 8,
            [shape((slots, out_cols)), shape((slots, out_cols), F32)],
            cost=(1e9, 3e6),
        )
    else:
        stacked = jnp.stack([latent, l1, l2, l3])
        lat = jnp.concatenate(
            [lax.dynamic_index_in_dim(stacked, t ^ i, 0, keepdims=False) for i in range(n_tp)], axis=1
        )
        lnorm = normed_rows(lat, lat_gain)
        used = lax.all_gather(totals[:1], "ctx", axis=0, tiled=True)
        rows_iota = jnp.arange(slots, dtype=jnp.int32)
        gather = lambda w, axis: lax.all_gather(w, "ctx", axis=axis, tiled=True)
        query = dot(lnorm, gather(query_proj, 0)).astype(BF16)
        kv = jnp.concatenate([dot(lnorm, gather(key_proj, 0)), dot(lnorm, gather(value_matrix, 0))], axis=1)
        keys = gather(kv.astype(BF16), 0)
        key_rows = jnp.arange(keys.shape[0], dtype=jnp.int32)
        allowed = (key_rows % slots < used[key_rows // slots])[None, :] & (
            key_rows[None, :] <= (c * slots + rows_iota)[:, None]
        )
        qh = jnp.transpose(query.reshape(slots, heads, HEAD_SIZE), (1, 0, 2))
        scores = jnp.einsum("hqd,kd->hqk", qh, keys[:, :kv_w], preferred_element_type=F32) / HEAD_SIZE**0.5
        scores = jnp.where(allowed[None], scores, NEG)
        expo = jnp.where(allowed[None], jnp.exp(scores - jnp.max(scores, axis=-1, keepdims=True)), 0.0)
        total = jnp.sum(expo, axis=-1, keepdims=True)
        mixed = jnp.einsum("hqk,kd->hqd", expo.astype(BF16), keys[:, kv_w:], preferred_element_type=F32) / total
        attn = jnp.transpose(mixed, (1, 0, 2)).reshape(slots, heads * HEAD_SIZE).astype(BF16)
        full = dot(attn, gather(out_proj, 1))
        pick = lambda j: lax.dynamic_slice_in_dim(full, (t ^ j) * out_cols, out_cols, 1)
        near_keep, near_send = pick(0), pick(1).astype(BF16)
        far_block = lambda j: lax.dynamic_slice_in_dim(full, (2 * (1 - a) + j) * out_cols, out_cols, 1)
        far0, far1 = [(far_block(j), far_block(j).astype(BF16)) for j in range(2)]

    far_recv = []
    for j, (full_block, low_block) in enumerate((far0, far1)):
        got = lax.ppermute(low_block, "tp", [(i ^ 1, i) for i in range(n_tp) if i % 2 == j])
        far = call(far_kernel, place, (full_block, got), (None,) * 2, [shape((slots, out_cols))])[0]
        far_recv.append(lax.ppermute(far, "tp", [(i, i ^ 2) for i in range(n_tp) if i % 2 == j]))
    near_recv = swap(near_send)
    if paired:
        down_send, down_keep = call(
            down_kernel,
            place,
            (latent, near_keep, near_recv, *far_recv, down_proj, from_x[8], from_x[9], from_z[8], from_z[9]),
            (None,) * 10,
            [shape((slots, half)), shape((slots, half), F32)],
            scratch=[pltpu.VMEM((slots, lat_cols), BF16)],
            cost=(0.6e9, 4e6),
        )
    else:
        base = latent.astype(F32) + near_keep + near_recv.astype(F32)
        latent_out = (base + far_recv[0].astype(F32) + far_recv[1].astype(F32)).astype(BF16)
        full = dot(latent_out, gather(down_proj, 1))
        down_keep = lax.dynamic_slice_in_dim(full, k * half, half, 1)
        down_send = lax.dynamic_slice_in_dim(full, (1 - k) * half, half, 1).astype(BF16)

    chip_sum, chip_low, trailing = call(
        sum_kernel,
        place,
        (totals, down_keep, swap(down_send)),
        (SMEM_SPEC, None, None),
        [shape((slots, half), F32), shape((slots, half)), shape((1, half))],
    )
    sum_recv = cross(chip_low)
    ahead = lambda at: [(g * n_tp + at * 2 + j, (g + 1) * n_tp + j) for g in range(n_ctx - 1) for j in range(2)]
    carry0 = lax.ppermute(trailing, ("ctx", "tp"), ahead(0))
    carry1 = lax.ppermute(trailing, ("ctx", "tp"), ahead(1))
    kept, send = call(
        final_kernel,
        place,
        (hidden, chip_sum, sum_recv, slot_col, carry0, carry1),
        (None,) * 6,
        [shape((nbytes, half))] * 2,
        scratch=[pltpu.VMEM((2 * nbytes, half), BF16)],
        cost=(0.4e9, 3e6),
    )
    got = swap(send)
    return where_k(jnp.concatenate([kept, got], axis=1), jnp.concatenate([got, kept], axis=1))


def solution(mesh):
    placed = (
        P(("dp", "ctx", "tp"), None),
        P(("dp", "ctx", "tp")),
        P(),
        P(),
        P(),
        P("ctx", "tp"),
        P(),
        P("ctx", "tp"),
        P("ctx", "tp"),
        P("ctx", "tp"),
        P("tp", "ctx"),
        P("tp", "ctx"),
    )

    return jax.shard_map(local, mesh=mesh, in_specs=placed, out_specs=P(("dp", "ctx", "tp"), None), check_vma=False)
```

```python
import functools

import jax
import jax.numpy as jnp
from jax import lax
from jax.experimental import pallas as pl
from jax.experimental.pallas import tpu as pltpu
from jax.sharding import PartitionSpec as P


HB = 64
HEAD_SIZE = 128
WIN = 512
EPS = 1e-05
LEAD = 32
NEG = -1e30
VMEM_LIMIT = 24 << 20
S_CTX = "ctx"
S_DP = "dp"
S_TP = "tp"

F32 = jnp.float32
BF16 = jnp.bfloat16


def dot(a, b):
    return jnp.dot(a, b, preferred_element_type=F32)


def dot_nt(a, b):
    return lax.dot_general(a, b, (((1,), (1,)), ((), ())), preferred_element_type=F32)


def normed_rows(x, gain):
    floats = x.astype(F32)
    scale = lax.rsqrt(jnp.mean(floats * floats, axis=-1, keepdims=True) + EPS)
    return (floats * scale * gain).astype(BF16)


def call(body, ids, args, in_specs, outs, out_specs=None, grid=(1,), scratch=(), cost=(1e7, 1e6), limit=VMEM_LIMIT):
    whole = pl.BlockSpec(memory_space=pltpu.VMEM)
    flops, nbytes = cost
    return pl.pallas_call(
        body,
        out_shape=outs,
        grid_spec=pltpu.PrefetchScalarGridSpec(
            num_scalar_prefetch=1,
            grid=grid,
            in_specs=[whole if spec is None else spec for spec in in_specs],
            out_specs=[whole] * len(outs) if out_specs is None else out_specs,
            scratch_shapes=list(scratch),
        ),
        compiler_params=pltpu.CompilerParams(
            dimension_semantics=("arbitrary",) * len(grid), vmem_limit_bytes=limit
        ),
        cost_estimate=pl.CostEstimate(flops=int(flops), bytes_accessed=int(nbytes), transcendentals=0),
    )(ids, *args)


K, A, C, Z, PREV = range(5)
USED, LAST = range(2)
SMEM_SPEC = pl.BlockSpec(memory_space=pltpu.SMEM)


def rows_at(start, n):
    return pl.ds(pl.multiple_of(start, n), n)


def first_kernel(ids, emb, starts, key, value, up, head, starts_out, kv_out, up_out):
    n, lane = LEAD, 128
    floats = starts[...].astype(F32)
    starts_out[...] = floats.astype(BF16)
    head[:n, :] = emb[...]
    head[n:, :] = jnp.ones((head.shape[0] - n, head.shape[1]), BF16)
    head[n:, :lane] = jnp.broadcast_to(floats[:, :lane], (head.shape[0] - n, lane)).astype(BF16)
    up_out[...] = up[...]

    @pl.when(ids[Z] == 0)
    def _():
        kv_out[...] = key[...]

    @pl.when(ids[Z] != 0)
    def _():
        kv_out[...] = value[...]


def halves_kernel(ids, query, out, out_rest, down, q0, q1, o0, o1, o2, o3, d0, d1):
    w = q0.shape[1]
    q0[...] = query[:, :w]
    q1[...] = query[:, w:]
    w = o0.shape[1]
    n = o1.shape[0]
    o0[...] = out[:, :w]
    o1[...] = out[:n, w:]
    o2[...] = out[n:, w:]
    o3[...] = out_rest[...]
    n = d0.shape[0]
    d0[...] = down[:n]
    d1[...] = down[n:]


def join_kernel(ids, own, other, o_ref):
    n = own.shape[1]
    k = ids[K]
    o_ref[:, rows_at(k * n, n)] = own[...]
    o_ref[:, rows_at((1 - k) * n, n)] = other[...]


def meta_kernel(ids, mine, other, extra0, extra1, slot_row, slot_col, totals):
    n = mine.shape[1]
    a = ids[A]
    lane = 128
    upper = (
        lax.broadcasted_iota(jnp.int32, (lane, lane), 0) <= lax.broadcasted_iota(jnp.int32, (lane, lane), 1)
    ).astype(F32).astype(BF16)

    def prefix(starts):
        return dot(jnp.broadcast_to(starts, (8, lane)).astype(BF16), upper)[:1]

    row_mine, row_other = mine[...].astype(F32), other[...].astype(F32)
    total_mine, total_other = jnp.sum(row_mine), jnp.sum(row_other)
    base = jnp.zeros((1, 1), F32) + jnp.where(a == 1, total_other, 0.0)
    for j in range(n // lane):
        at = slice(j * lane, (j + 1) * lane)
        sums = prefix(row_mine[:, at]) + base
        slot_row[:, at] = sums.astype(jnp.int32) - 1
        base = sums[:, lane - 1 :]
    own_used = (total_mine + total_other).astype(jnp.int32)
    follow = (extra0[LEAD:, :] + extra1[LEAD:, :])[:1].astype(F32)
    led = prefix(follow[:, :lane])[:, :LEAD]
    leads = (led < 0.5) & (follow[:, lane : lane + 1] > 0.5)
    slot_row[:, n:] = jnp.where(leads, own_used - 1, -1)
    row = lax.broadcasted_iota(jnp.int32, (n, n), 0)
    col = lax.broadcasted_iota(jnp.int32, (n, n), 1)
    slot_col[...] = jnp.sum(jnp.where(row == col, slot_row[:, :n].astype(F32), 0.0), axis=1, keepdims=True).astype(
        jnp.int32
    )
    totals[USED] = own_used
    totals[LAST] = own_used - 1


def qkv_kernel(ids, own, other, extra0, extra1, gain, w_hbm, q_ref, kt_ref, kx_ref, v_ref, wk, wv, normed, wq, sems):
    n, width = own.shape
    half = width // 2
    k = ids[K]
    copies = []
    for part, target in ((1, wk), (2, wv), (0, wq)):
        at = pl.ds(pl.multiple_of(part * width + k * half, half), half)
        copies.append(pltpu.make_async_copy(w_hbm.at[:, at], target, sems.at[part]))
        copies[-1].start()
    normed[rows_at(k * n, n), :] = normed_rows(own[...], gain[...])
    normed[rows_at((1 - k) * n, n), :] = normed_rows(other[...], gain[...])
    normed[2 * n :, :] = normed_rows(extra0[:LEAD, :] + extra1[:LEAD, :], gain[...])
    for copy in copies:
        copy.wait()
    w = 256
    for j in range(half // w):
        at = slice(j * w, (j + 1) * w)
        keys = dot(normed[...], wk[:, at])
        kx_ref[:, at] = keys[2 * n :].astype(BF16)
        kt_ref[at, :] = jnp.transpose(keys[: 2 * n]).astype(BF16)
        v_ref[:, at] = dot(normed[...], wv[:, at]).astype(BF16)
        q_ref[:, at] = (dot(normed[...], wq[:, at]).astype(BF16).astype(F32) * (1.0 / HB**0.5)).astype(BF16)


def halo_kernel(ids, own, other, gain, normed):
    n = own.shape[0]
    k = ids[K]
    normed[rows_at(k * n, n), :] = normed_rows(own[...], gain[...])
    normed[rows_at((1 - k) * n, n), :] = normed_rows(other[...], gain[...])


def window_kernel(ids, normed, wk, wv, q_ref, kt_ref, kx_ref, v_ref, o_ref, kht, vh, *, g):
    n = normed.shape[0] // 2
    rows = 2 * n
    n_extra = q_ref.shape[0] - rows
    blk = 128
    lanes = 2 * HB
    nblk = rows // blk
    bias = jnp.where(ids[PREV] == 1, 0.0, NEG).astype(F32)
    low = lax.broadcasted_iota(jnp.int32, (blk, lanes), 1) < HB
    r = lax.broadcasted_iota(jnp.int32, (2 * blk, blk), 0)
    causal = lax.broadcasted_iota(jnp.int32, (2 * blk, blk), 1) <= jnp.where(r >= blk, r - blk, r)
    re = lax.broadcasted_iota(jnp.int32, (2 * n_extra, rows), 0)
    re = jnp.where(re >= n_extra, re - n_extra, re)
    ok_own = lax.broadcasted_iota(jnp.int32, (2 * n_extra, rows), 1) > re
    ok_new = lax.broadcasted_iota(jnp.int32, (2 * n_extra, n_extra), 1) <= re[:, :n_extra]

    def split(qb):
        keep = low[: qb.shape[0]]
        none = jnp.zeros_like(qb)
        return jnp.concatenate([jnp.where(keep, qb, none), jnp.where(keep, none, qb)], axis=0)

    def join(mixed):
        m = mixed.shape[0] // 2
        mixed = mixed[:, :lanes] / mixed[:, lanes:]
        return jnp.where(low[:m], mixed[:m], mixed[m:]).astype(BF16)

    def weighted(e, v):
        return dot(e.astype(BF16), jnp.concatenate([v, jnp.ones_like(v)], axis=1))

    w = kht.shape[0]
    wide = slice(g * w, (g + 1) * w)
    kht[...] = jnp.transpose(dot(normed[...], wk[:, wide])).astype(BF16)
    vh[...] = dot(normed[...], wv[:, wide]).astype(BF16)
    for pair in range(w // lanes):
        cols = slice(g * w + pair * lanes, g * w + (pair + 1) * lanes)
        part = slice(pair * lanes, (pair + 1) * lanes)
        for b in range(nblk):
            q2 = split(q_ref[b * blk : (b + 1) * blk, cols])
            s_own = dot(q2, kt_ref[cols, : (b + 1) * blk])
            s_halo = dot(q2, kht[part, b * blk :]) + bias
            diag = jnp.where(causal, s_own[:, b * blk :], s_halo[:, :blk])
            peak = jnp.max(diag, axis=-1, keepdims=True)
            if b > 0:
                peak = jnp.maximum(peak, jnp.max(s_own[:, : b * blk], axis=-1, keepdims=True))
            if b < nblk - 1:
                peak = jnp.maximum(peak, jnp.max(s_halo[:, blk:], axis=-1, keepdims=True))
            e_diag = jnp.exp(diag - peak)
            e_own = jnp.where(causal, e_diag, 0.0)
            e_halo = jnp.where(causal, 0.0, e_diag)
            if b > 0:
                e_own = jnp.concatenate([jnp.exp(s_own[:, : b * blk] - peak), e_own], axis=1)
            if b < nblk - 1:
                e_halo = jnp.concatenate([e_halo, jnp.exp(s_halo[:, blk:] - peak)], axis=1)
            mixed = weighted(e_own, v_ref[: (b + 1) * blk, cols]) + weighted(e_halo, vh[b * blk :, part])
            o_ref[b * blk : (b + 1) * blk, part] = join(mixed)
        q2 = split(q_ref[rows:, cols])
        s_own = jnp.where(ok_own, dot(q2, kt_ref[cols, :]), NEG)
        s_new = jnp.where(ok_new, dot_nt(q2, kx_ref[:, cols]), NEG)
        peak = jnp.maximum(jnp.max(s_own, axis=-1, keepdims=True), jnp.max(s_new, axis=-1, keepdims=True))
        mixed = weighted(jnp.exp(s_own - peak), v_ref[:rows, cols]) + weighted(
            jnp.exp(s_new - peak), v_ref[rows:, cols]
        )
        o_ref[rows:, part] = join(mixed)


def hidden_kernel(ids, own0, own1, other0, other1, w_out, emb_own, emb_other, extra0, extra1, slot, h_ref, p_ref, n_ref, send, acc):
    n = emb_own.shape[0]
    half = acc.shape[1]
    k = ids[K]
    mine = pl.ds(pl.multiple_of(k * half, half), half)
    acc[rows_at(k * n, n), :] = emb_own[:, mine].astype(F32)
    acc[rows_at((1 - k) * n, n), :] = emb_other[:, mine].astype(F32)
    acc[2 * n :, :] = (extra0[:LEAD, mine] + extra1[:LEAD, mine]).astype(F32)
    w = own0.shape[1]
    mixed = 0.0
    for at, shift, piece in ((k, 0, own0), (k, w, own1), (1 - k, 0, other0), (1 - k, w, other1)):
        mixed = mixed + dot(piece[...], w_out[rows_at(at * half + shift, w), mine])
    hidden = (acc[...] + mixed).astype(BF16)
    h_ref[...] = hidden[: 2 * n]
    hot = (lax.broadcasted_iota(jnp.int32, (p_ref.shape[0], acc.shape[0]), 0) == slot[...]).astype(F32)
    count = jnp.broadcast_to(jnp.sum(hot, axis=1, keepdims=True), n_ref.shape)
    part = dot(hot.astype(BF16), hidden)
    p_ref[...] = part
    n_ref[...] = count
    send[:, :half] = part.astype(BF16)
    send[:, half:] = count.astype(BF16)


def pool_kernel(ids, part, count, recv, o_ref):
    half = part.shape[1]
    total = part[...] + recv[:, :half].astype(F32)
    number = count[:, :1] + recv[:, half : half + 1].astype(F32)
    o_ref[...] = (total / jnp.maximum(number, 1.0)).astype(BF16)


def up_kernel(ids, half, other, w_own, w_x, w_z, o_ref, pool):
    n = half.shape[1]
    k, c, z = ids[K], ids[C], ids[Z]
    pool[:, pl.ds(pl.multiple_of(k * n, n), n)] = half[...]
    pool[:, pl.ds(pl.multiple_of((1 - k) * n, n), n)] = other[...]
    rows = w_own.shape[0]
    part = rows // 2
    own = dot(pool[:, pl.ds(pl.multiple_of(c * rows, rows), rows)], w_own[...])
    base = (1 - c) * rows
    at_x = pl.multiple_of(base + z * part, part)
    at_z = pl.multiple_of(base + (1 - z) * part, part)
    total = own + dot(pool[:, pl.ds(at_x, part)], w_x[...]) + dot(pool[:, pl.ds(at_z, part)], w_z[...])
    o_ref[...] = total.astype(BF16)


def kv_kernel(ids, totals, l0, l1, l2, l3, gain, wk, wv, w_x, w_z, s_ref, scale_ref, kv_ref):
    n = l0.shape[1]
    t = ids[A] * 2 + ids[K]
    step = 32

    def rows_step(i, _):
        rows = pl.ds(pl.multiple_of(i * step, step), step)
        square = jnp.zeros((step, 1), F32)
        for j, piece in enumerate((l0, l1, l2, l3)):
            at = pl.multiple_of((t ^ j) * n, n)
            floats = piece[rows, :].astype(F32)
            square = square + jnp.sum(floats * floats, axis=-1, keepdims=True)
            s_ref[rows, pl.ds(at, n)] = (floats * gain[:, pl.ds(at, n)]).astype(BF16)
        scale_ref[rows, :] = jnp.broadcast_to(lax.rsqrt(square / (4 * n) + EPS), (step, scale_ref.shape[1]))
        return 0

    lax.fori_loop(0, l0.shape[0] // step, rows_step, 0)
    scale = scale_ref[:, :1]
    rows = wk.shape[0]
    c, z = ids[C], ids[Z]
    mine = s_ref[:, pl.ds(pl.multiple_of(c * rows, rows), rows)]
    base = (1 - c) * rows
    rest = s_ref[:, rows_at(base, rows)]
    slots = l0.shape[0]
    w = wk.shape[1]
    for parity, key, value in ((0, w_x, w_z), (1, w_z, w_x)):

        @pl.when(z == parity)
        def _(key=key, value=value):
            kv_ref[:slots, :w] = ((dot(mine, wk[...]) + dot(rest, key[...])) * scale).astype(BF16)
            kv_ref[:slots, w:] = ((dot(mine, wv[...]) + dot(rest, value[...])) * scale).astype(BF16)

    count = jnp.zeros((kv_ref.shape[0] - slots, 2 * w), F32) + totals[USED].astype(F32)
    kv_ref[slots:, :] = count.astype(BF16)


def q_kernel(ids, s_ref, scale, w_own, x0, z0, x1, z1, q_ref):
    rows = w_own.shape[0]
    part = rows // 2
    w = x0.shape[1]
    c, z = ids[C], ids[Z]
    base = (1 - c) * rows
    mine = s_ref[:, pl.ds(pl.multiple_of(c * rows, rows), rows)]
    sx = s_ref[:, pl.ds(pl.multiple_of(base + z * part, part), part)]
    sz = s_ref[:, pl.ds(pl.multiple_of(base + (1 - z) * part, part), part)]
    for j, (wx, wz) in enumerate(((x0, z0), (x1, z1))):
        total = dot(mine, w_own[:, j * w : (j + 1) * w]) + dot(sx, wx[...]) + dot(sz, wz[...])
        q_ref[:, j * w : (j + 1) * w] = (total * scale[:, :1]).astype(BF16)


def latent_attend(ids, totals, q_ref, kv_own, kv_other, attn):
    slots = q_ref.shape[0]
    d = HEAD_SIZE
    blk = 128
    scale = 1.0 / HEAD_SIZE**0.5
    col = lax.broadcasted_iota(jnp.int32, (blk, slots), 1)
    row = lax.broadcasted_iota(jnp.int32, (blk, slots), 0)
    used_other = kv_other[slots:, :][:1, :1].astype(F32)
    ok_other = col.astype(F32) < jnp.where(ids[C] == 1, used_other, 0.0)
    ones = jnp.ones((slots, d), BF16)
    v_own = jnp.concatenate([kv_own[:slots, d:], ones], axis=1)
    v_other = jnp.concatenate([kv_other[:slots, d:], ones], axis=1)
    for b in range(slots // blk):
        ok_own = (col <= row + b * blk) & (col < totals[USED])
        for h in range(q_ref.shape[1] // d):
            qh = q_ref[b * blk : (b + 1) * blk, h * d : (h + 1) * d]
            s0 = jnp.where(ok_own, dot_nt(qh, kv_own[:slots, :d]) * scale, NEG)
            s1 = jnp.where(ok_other, dot_nt(qh, kv_other[:slots, :d]) * scale, NEG)
            peak = jnp.maximum(jnp.max(s0, axis=-1, keepdims=True), jnp.max(s1, axis=-1, keepdims=True))
            e0 = jnp.exp(s0 - peak).astype(BF16)
            e1 = jnp.exp(s1 - peak).astype(BF16)
            mixed = dot(e0, v_own) + dot(e1, v_other)
            attn[b * blk : (b + 1) * blk, h * d : (h + 1) * d] = (mixed[:, :d] / mixed[:, d:]).astype(BF16)


def blocks_of(attn, w_own, x0, z0, pieces, chip, c, z, store, which):
    w, part = x0.shape[1], x0.shape[0]

    @pl.when(chip == c)
    def _():
        for j in which:
            store(j, dot(attn[...], w_own[:, j * w : (j + 1) * w]))

    @pl.when(chip != c)
    def _():
        at_x, at_z = z * part, (1 - z) * part
        if 0 in which:
            store(0, dot(attn[:, rows_at(at_x, part)], x0[...]) + dot(attn[:, rows_at(at_z, part)], z0[...]))
        if 1 in which:
            n = part // 2
            total = 0.0
            for at, piece in zip((at_x, at_x + n, at_z + n, at_z), pieces):
                total = total + dot(attn[:, rows_at(at, n)], piece[...])
            store(1, total)


def attend_kernel(ids, totals, q_ref, kv_own, kv_other, attn):
    latent_attend(ids, totals, q_ref, kv_own, kv_other, attn)


def far0_kernel(ids, attn, w_own, x0, z0, full, low):
    def store(j, value):
        full[...] = value
        low[...] = value.astype(BF16)

    blocks_of(attn, w_own, x0, z0, (), 1 - ids[A], ids[C], ids[Z], store, (0,))


def far1_kernel(ids, attn, w_own, x0, x1, x2, x3, z1, full, low):
    def store(j, value):
        full[...] = value
        low[...] = value.astype(BF16)

    blocks_of(attn, w_own, x0, None, (x1, x2, x3, z1), 1 - ids[A], ids[C], ids[Z], store, (1,))


def near_kernel(ids, attn, w_own, x0, z0, x1, x2, x3, z1, send, keep):
    k = ids[K]

    def store(j, value):
        @pl.when(k == j)
        def _():
            keep[...] = value.astype(keep.dtype)

        @pl.when(k != j)
        def _():
            send[...] = value.astype(send.dtype)

    blocks_of(attn, w_own, x0, z0, (x1, x2, x3, z1), ids[A], ids[C], ids[Z], store, (0, 1))


def far_kernel(ids, keep, recv, o_ref):
    o_ref[...] = (keep[...] + recv[...].astype(F32)).astype(BF16)


def down_kernel(ids, latent, near_keep, near_recv, far0, far1, w_own, x0, x1, z0, z1, send, keep, lo):
    k, c, z = ids[K], ids[C], ids[Z]
    near = latent[...].astype(F32) + near_keep[...] + near_recv[...].astype(F32)
    lo[...] = (near + far0[...].astype(F32) + far1[...].astype(F32)).astype(BF16)
    n = x0.shape[0]
    part = 2 * n
    own = dot(lo[...], w_own[...])
    at_x, at_z = z * part, (1 - z) * part
    rest = 0.0
    for at, piece in ((at_x, x0), (at_x + n, x1), (at_z, z0), (at_z + n, z1)):
        rest = rest + dot(lo[:, rows_at(at, n)], piece[...])

    @pl.when(c == k)
    def _():
        keep[...] = own
        send[...] = rest.astype(BF16)

    @pl.when(c != k)
    def _():
        keep[...] = rest
        send[...] = own.astype(BF16)


def sum_kernel(ids, totals, keep, recv, full, low, trailing):
    full[...] = keep[...] + recv[...].astype(F32)
    low[...] = full[...].astype(BF16)
    trailing[...] = full[pl.ds(totals[LAST], 1), :].astype(BF16)


def final_kernel(ids, hidden, patch, recv, slot, carry0, carry1, kept, send, states):
    patch_out = (patch[...] + recv[...].astype(F32)).astype(BF16)
    rows = hidden.shape[0]
    n = rows // 2
    hot = lax.broadcasted_iota(jnp.int32, (rows, patch.shape[0]), 1) == slot[...]
    spread = dot(hot.astype(F32).astype(BF16), patch_out)
    carried = (carry0[...].astype(F32) + carry1[...].astype(F32)).astype(BF16).astype(F32)
    lead = (slot[...] < 0).astype(F32)
    states[...] = (hidden[...].astype(F32) + spread + lead * carried).astype(BF16)
    k = ids[K]
    kept[...] = states[rows_at(k * n, n), :]
    send[...] = states[rows_at((1 - k) * n, n), :]


def shape(dims, dtype=BF16):
    return jax.ShapeDtypeStruct(dims, dtype)


def local(
    byte_embed,
    patch_start,
    enc_gain,
    enc_qkv,
    enc_out,
    up_proj,
    lat_gain,
    query_proj,
    key_proj,
    value_matrix,
    out_proj,
    down_proj,
):
    nbytes, width = byte_embed.shape
    n_tp = lax.axis_size(S_TP)
    n_ctx = lax.axis_size(S_CTX)
    n_dp = lax.axis_size(S_DP)
    assert 2 * nbytes == WIN and n_tp == 4
    half = width // 2
    slots = n_tp * nbytes // 4
    t = lax.axis_index(S_TP)
    c = lax.axis_index(S_CTX)
    zp = lax.axis_index(S_DP) % 2
    a, k = t // 2, t % 2
    where_k = lambda first, second: jnp.where(k == 0, first, second)

    def swap(x):
        return lax.ppermute(x, S_TP, [(i, i ^ 1) for i in range(n_tp)])

    def cross(x):
        return lax.ppermute(x, S_TP, [(i, i ^ 2) for i in range(n_tp)])

    def forward(x):
        n = n_ctx * n_tp
        return lax.ppermute(x, (S_CTX, S_TP), [(i, i + 2) for i in range(n - 2)])

    def flip(x):
        return lax.ppermute(x, S_CTX, [(0, 1), (1, 0)])

    def pair(x):
        return lax.ppermute(x, S_DP, [(i, i ^ 1) for i in range(n_dp)])

    paired = n_ctx == 2

    emb_halo = forward(byte_embed)
    emb_other = swap(byte_embed)
    emb_halo_other = swap(emb_halo)

    one = lambda x: x.astype(jnp.int32)
    place = jnp.stack([one(k), one(a), one(c), one(zp), one(c * 2 + a > 0)])

    in_hbm = lambda x: pltpu.with_memory_space_constraint(x, pltpu.HBM)

    up_rows = up_proj.shape[0] // 2
    block_of = lambda rows, cols, at: pl.BlockSpec((rows, cols), lambda p, ids: (at(ids), 0))
    origin = lambda ids: 0
    head, starts, kv_piece, up_piece = call(
        first_kernel,
        place,
        (in_hbm(byte_embed), in_hbm(patch_start.reshape(1, nbytes)), in_hbm(key_proj), in_hbm(value_matrix), in_hbm(up_proj)),
        [
            block_of(LEAD, width, origin),
            block_of(1, nbytes, origin),
            block_of(*key_proj.shape, origin),
            block_of(*value_matrix.shape, origin),
            block_of(up_rows, up_proj.shape[1], lambda ids: ids[Z]),
        ],
        [shape((LEAD + 16, width)), shape((1, nbytes)), shape(key_proj.shape), shape((up_rows, up_proj.shape[1]))],
        cost=(1e6, 3e6),
    )
    extras = []
    for j in range(2):
        extras.append(
            lax.ppermute(head, (S_CTX, S_TP), [(g * n_tp, g * n_tp - 2 + j) for g in range(1, n_ctx)])
        )

    chip_starts = call(join_kernel, place, (starts, swap(starts)), (None,) * 2, [shape((1, 2 * nbytes))])[0]
    chip_far = cross(chip_starts)
    slot_row, slot_col, totals = call(
        meta_kernel,
        place,
        (chip_starts, chip_far, *extras),
        (None,) * 4,
        [shape((1, 2 * nbytes + LEAD), jnp.int32), shape((2 * nbytes, 1), jnp.int32), shape((2,), jnp.int32)],
        [pl.BlockSpec(memory_space=pltpu.VMEM)] * 2 + [SMEM_SPEC],
    )

    if paired:
        rows = lambda w: w.shape[0] // 2
        part = lambda w: pl.BlockSpec((rows(w), w.shape[1]), lambda p, ids: (ids[Z], 0))
        q_cols, o_cols = query_proj.shape[1] // 2, out_proj.shape[1] // 2
        q_rows, o_rows = rows(query_proj), rows(out_proj)
        sizes = [
            *[(q_rows, q_cols)] * 2,
            (o_rows, o_cols),
            *[(o_rows // 2, o_cols)] * 3,
            *[(rows(down_proj) // 2, down_proj.shape[1])] * 2,
        ]

        o_rest = pl.BlockSpec((o_rows // 2, o_cols), lambda p, ids: (2 * (1 - ids[Z]) + 1, 1))
        pieces = [up_piece, kv_piece]
        pieces += call(
            halves_kernel,
            place,
            (query_proj, out_proj, out_proj, down_proj),
            [part(query_proj), part(out_proj), o_rest, part(down_proj)],
            [shape(d) for d in sizes],
            [pl.BlockSpec(d, lambda p, ids: (0, 0)) for d in sizes],
            cost=(1e6, 5e6),
        )
        from_x = [flip(p) for p in pieces]
        from_z = [pair(p) if i not in (6, 7) else None for i, p in enumerate(from_x)]

    gain = enc_gain.reshape(1, width)
    n_rows = 2 * nbytes + LEAD
    q, kt, kx, v, wk, wv = call(
        qkv_kernel,
        place,
        (byte_embed, emb_other, *extras, gain, in_hbm(enc_qkv)),
        (None, None, None, None, None, pl.BlockSpec(memory_space=pltpu.HBM)),
        [
            shape((n_rows, half)),
            shape((half, 2 * nbytes)),
            shape((LEAD, half)),
            shape((n_rows, half)),
            shape((width, half)),
            shape((width, half)),
        ],
        scratch=[
            pltpu.VMEM((n_rows, width), BF16),
            pltpu.VMEM((width, half), BF16),
            pltpu.SemaphoreType.DMA((3,)),
        ],
        cost=(2 * n_rows * width * 3 * half, 3e6),
    )
    normed = call(
        halo_kernel, place, (emb_halo, emb_halo_other, gain), (None,) * 3, [shape((2 * nbytes, width))], cost=(1e7, 2e6)
    )[0]
    context, context_other = [], []
    for g in range(half // 256):
        context.append(
            call(
                functools.partial(window_kernel, g=g),
                place,
                (normed, wk, wv, q, kt, kx, v),
                (None,) * 7,
                [shape((n_rows, 256))],
                scratch=[pltpu.VMEM((256, 2 * nbytes), BF16), pltpu.VMEM((2 * nbytes, 256), BF16)],
                cost=(4e9, 3e6),
            )[0]
        )
        context_other.append(swap(context[-1]))
    hidden, part_sum, part_count, part_send = call(
        hidden_kernel,
        place,
        (*context, *context_other, enc_out, byte_embed, emb_other, *extras, slot_row),
        (None,) * 10,
        [
            shape((2 * nbytes, half)),
            shape((slots, half), F32),
            shape((slots, 128), F32),
            shape((slots, half + 128)),
        ],
        scratch=[pltpu.VMEM((n_rows, half), F32)],
        cost=(1.5e9, 4e6),
    )

    part_recv = cross(part_send)
    pooled = call(pool_kernel, place, (part_sum, part_count, part_recv), (None,) * 3, [shape((slots, half))])[0]
    pooled_other = swap(pooled)

    out_cols = out_proj.shape[1] * n_ctx // n_tp
    lat_cols = up_proj.shape[1]
    if paired:
        latent = call(
            up_kernel,
            place,
            (pooled, pooled_other, up_proj, from_x[0], from_z[0]),
            (None,) * 5,
            [shape((slots, lat_cols))],
            scratch=[pltpu.VMEM((slots, width), BF16)],
            cost=(0.6e9, 4e6),
        )[0]
    else:
        whole = where_k(
            jnp.concatenate([pooled, pooled_other], axis=1), jnp.concatenate([pooled_other, pooled], axis=1)
        )
        latent = dot(whole, lax.all_gather(up_proj, S_CTX, axis=0, tiled=True)).astype(BF16)

    l2 = cross(latent)
    l1 = swap(latent)
    l3 = swap(l2)
    heads = query_proj.shape[1] // HEAD_SIZE
    kv_w = key_proj.shape[1]
    if paired:
        scaled, scale, kv = call(
            kv_kernel,
            place,
            (totals, latent, l1, l2, l3, lat_gain.reshape(1, -1), key_proj, value_matrix, from_x[1], from_z[1]),
            (SMEM_SPEC, *(None,) * 9),
            [shape((slots, 4 * lat_cols)), shape((slots, 128), F32), shape((slots + 16, 2 * kv_w))],
            cost=(1e9, 6e6),
        )
        kv_far = flip(kv)
        query = call(
            q_kernel,
            place,
            (scaled, scale, query_proj, from_x[2], from_z[2], from_x[3], from_z[3]),
            (None,) * 7,
            [shape((slots, heads * HEAD_SIZE))],
            cost=(1.2e9, 6e6),
        )[0]
        attn = call(
            attend_kernel,
            place,
            (totals, query, kv, kv_far),
            (SMEM_SPEC, None, None, None),
            [shape((slots, heads * HEAD_SIZE))],
            cost=(5e8, 1e6),
        )[0]
        o1 = (from_x[5], from_x[6], from_x[7], from_z[5])
        block_out = [shape((slots, out_cols), F32), shape((slots, out_cols))]
        far0 = call(far0_kernel, place, (attn, out_proj, from_x[4], from_z[4]), (None,) * 4, block_out, cost=(3e8, 2e6))
        far1 = call(far1_kernel, place, (attn, out_proj, from_x[4], *o1), (None,) * 7, block_out, cost=(3e8, 2e6))
        near_send, near_keep = call(
            near_kernel,
            place,
            (attn, out_proj, from_x[4], from_z[4], *o1),
            (None,) * 8,
            [shape((slots, out_cols)), shape((slots, out_cols), F32)],
            cost=(1e9, 3e6),
        )
    else:
        stacked = jnp.stack([latent, l1, l2, l3])
        lat = jnp.concatenate(
            [lax.dynamic_index_in_dim(stacked, t ^ i, 0, keepdims=False) for i in range(n_tp)], axis=1
        )
        lnorm = normed_rows(lat, lat_gain)
        used = lax.all_gather(totals[:1], S_CTX, axis=0, tiled=True)
        rows_iota = jnp.arange(slots, dtype=jnp.int32)
        gather = lambda w, axis: lax.all_gather(w, S_CTX, axis=axis, tiled=True)
        query = dot(lnorm, gather(query_proj, 0)).astype(BF16)
        kv = jnp.concatenate([dot(lnorm, gather(key_proj, 0)), dot(lnorm, gather(value_matrix, 0))], axis=1)
        keys = gather(kv.astype(BF16), 0)
        key_rows = jnp.arange(keys.shape[0], dtype=jnp.int32)
        allowed = (key_rows % slots < used[key_rows // slots])[None, :] & (
            key_rows[None, :] <= (c * slots + rows_iota)[:, None]
        )
        qh = jnp.transpose(query.reshape(slots, heads, HEAD_SIZE), (1, 0, 2))
        scores = jnp.einsum("hqd,kd->hqk", qh, keys[:, :kv_w], preferred_element_type=F32) / HEAD_SIZE**0.5
        scores = jnp.where(allowed[None], scores, NEG)
        expo = jnp.where(allowed[None], jnp.exp(scores - jnp.max(scores, axis=-1, keepdims=True)), 0.0)
        total = jnp.sum(expo, axis=-1, keepdims=True)
        mixed = jnp.einsum("hqk,kd->hqd", expo.astype(BF16), keys[:, kv_w:], preferred_element_type=F32) / total
        attn = jnp.transpose(mixed, (1, 0, 2)).reshape(slots, heads * HEAD_SIZE).astype(BF16)
        full = dot(attn, gather(out_proj, 1))
        pick = lambda j: lax.dynamic_slice_in_dim(full, (t ^ j) * out_cols, out_cols, 1)
        near_keep, near_send = pick(0), pick(1).astype(BF16)
        far_block = lambda j: lax.dynamic_slice_in_dim(full, (2 * (1 - a) + j) * out_cols, out_cols, 1)
        far0, far1 = [(far_block(j), far_block(j).astype(BF16)) for j in range(2)]

    far_recv = []
    for j, (full_block, low_block) in enumerate((far0, far1)):
        got = lax.ppermute(low_block, S_TP, [(i ^ 1, i) for i in range(n_tp) if i % 2 == j])
        far = call(far_kernel, place, (full_block, got), (None,) * 2, [shape((slots, out_cols))])[0]
        far_recv.append(lax.ppermute(far, S_TP, [(i, i ^ 2) for i in range(n_tp) if i % 2 == j]))
    near_recv = swap(near_send)
    if paired:
        down_send, down_keep = call(
            down_kernel,
            place,
            (latent, near_keep, near_recv, *far_recv, down_proj, from_x[8], from_x[9], from_z[8], from_z[9]),
            (None,) * 10,
            [shape((slots, half)), shape((slots, half), F32)],
            scratch=[pltpu.VMEM((slots, lat_cols), BF16)],
            cost=(0.6e9, 4e6),
        )
    else:
        base = latent.astype(F32) + near_keep + near_recv.astype(F32)
        latent_out = (base + far_recv[0].astype(F32) + far_recv[1].astype(F32)).astype(BF16)
        full = dot(latent_out, gather(down_proj, 1))
        down_keep = lax.dynamic_slice_in_dim(full, k * half, half, 1)
        down_send = lax.dynamic_slice_in_dim(full, (1 - k) * half, half, 1).astype(BF16)

    chip_sum, chip_low, trailing = call(
        sum_kernel,
        place,
        (totals, down_keep, swap(down_send)),
        (SMEM_SPEC, None, None),
        [shape((slots, half), F32), shape((slots, half)), shape((1, half))],
    )
    sum_recv = cross(chip_low)
    ahead = lambda at: [(g * n_tp + at * 2 + j, (g + 1) * n_tp + j) for g in range(n_ctx - 1) for j in range(2)]
    carry0 = lax.ppermute(trailing, (S_CTX, S_TP), ahead(0))
    carry1 = lax.ppermute(trailing, (S_CTX, S_TP), ahead(1))
    kept, send = call(
        final_kernel,
        place,
        (hidden, chip_sum, sum_recv, slot_col, carry0, carry1),
        (None,) * 6,
        [shape((nbytes, half))] * 2,
        scratch=[pltpu.VMEM((2 * nbytes, half), BF16)],
        cost=(0.4e9, 3e6),
    )
    got = swap(send)
    return where_k(jnp.concatenate([kept, got], axis=1), jnp.concatenate([got, kept], axis=1))


def solution(mesh):
    placed = (
        P((S_DP, S_CTX, S_TP), None),
        P((S_DP, S_CTX, S_TP)),
        P(),
        P(),
        P(),
        P(S_CTX, S_TP),
        P(),
        P(S_CTX, S_TP),
        P(S_CTX, S_TP),
        P(S_CTX, S_TP),
        P(S_TP, S_CTX),
        P(S_TP, S_CTX),
    )

    return jax.shard_map(local, mesh=mesh, in_specs=placed, out_specs=P((S_DP, S_CTX, S_TP), None), check_vma=False)
```
